32 devices in a mesh: dp: 8 (over z, y), mp: 4 (over x, core).
Axes of the slice: x: 2, y: 2, z: 4, core: 2. Of those that a mesh axis runs over, the one named last changes fastest.
Arguments:
- patches: bfloat16 [16384, 1024], P('dp'), may hold values from -110 to 110
- dest_owner: int32 [1024], P('dp'), may hold values from 0 to 7, as said below
- dest_slot: int32 [1024], P('dp'), may hold values from 0 to 127
- packed_image: int32 [1024], P('dp'), may hold values from -1 to 15, as said below
- w_query: bfloat16 [1024, 1024], P(None, 'mp'), may hold values from -0.328125 to 0.328125
- w_key: bfloat16 [1024, 1024], P(None, 'mp'), may hold values from -1.9375 to 1.9375
- w_value: bfloat16 [1024, 1024], P(None, 'mp'), may hold values from -0.1875 to 0.1875
- w_out: bfloat16 [1024, 1024], P('mp'), may hold values from -0.1875 to 0.1875
Outputs:
- packed_out: bfloat16 [16384, 1024], P('dp', 'mp')
- pooled_out: bfloat16 [128, 1024], P('dp', 'mp')
The draws below stay inside these ranges and needn't reach their ends.
Inputs may be any that keep to these rules, and one draw needn't show every extreme that they name: dest_owner and dest_slot take the tiles of all indices of dp one to one onto the 128 tile slots of every packed sequence; each index of dp holds exactly 16 tiles for each packed sequence. `packed_image`: in every packed sequence the images 0, 1, 2 and so on lie on consecutive tile slots from slot 0 in the order of their numbers, each on 8 to 16 slots; fewer than 16 slots stay empty after the last image and hold -1.
All inputs are finite; a program needn't handle non-finite values.
Results may differ from the reference program's by a relative error of at most 0.0075.
Values may be sent and summed in bfloat16 or wider, within the bound.
A program may use at most 128 MiB of HBM per device.

```python
import math
import jax
import jax.numpy as jnp
from jax import lax

D = 1024
HEADS = 16
HEAD_DIM = 64
TILE = 16
MAXT = 16
MINT = 8
SLOTS = 128
IMG_OWN = 16
ROWS = 16384
N_DP = 8
N_MP = 4


def layout(key):
    per_pair = SLOTS // N_DP
    owner_keys = jax.random.split(jax.random.fold_in(key, 101), N_DP)
    source_keys = jax.random.split(jax.random.fold_in(key, 102), N_DP)
    slot_perm = jax.vmap(lambda single: jax.random.permutation(single, SLOTS))(owner_keys).astype(jnp.int32)
    tile_perm = jax.vmap(lambda single: jax.random.permutation(single, SLOTS))(source_keys).astype(jnp.int32)
    sources = jnp.arange(N_DP, dtype=jnp.int32)[:, None]
    owners = tile_perm // per_pair
    within = tile_perm % per_pair
    column = (sources - owners) % N_DP + N_DP * within
    slots = slot_perm[owners, column]
    owner_ids = jnp.arange(N_DP, dtype=jnp.int32)
    image_tiles = jax.random.randint(jax.random.fold_in(key, 104), (N_DP, IMG_OWN), MINT, MAXT + 1)
    biggest = jax.random.randint(jax.random.fold_in(key, 105), (), 0, N_DP)
    fullest = (biggest + 1) % N_DP
    image_tiles = jnp.where((owner_ids == fullest)[:, None], MINT, image_tiles)
    image_tiles = image_tiles.at[:, 0].set(jnp.where(owner_ids == biggest, MAXT, image_tiles[:, 0]))
    kept = jnp.cumsum(image_tiles, axis=1) <= SLOTS
    image_tiles = jnp.where(kept, image_tiles, 0)
    ends = jnp.cumsum(image_tiles, axis=1)
    tile_ids = jnp.arange(SLOTS, dtype=jnp.int32)
    finished = jnp.sum((tile_ids[None, :, None] >= ends[:, None, :]).astype(jnp.int32), axis=2)
    image = jnp.where(tile_ids[None, :] < ends[:, -1:], finished, -1)
    return (owners.reshape(-1).astype(jnp.int32), slots.reshape(-1).astype(jnp.int32), image.reshape(-1).astype(jnp.int32))


def draw_dest_owner(key, part):
    return layout(key)[0]


def draw_dest_slot(key, part):
    return layout(key)[1]


def draw_packed_image(key, part):
    return layout(key)[2]


def draw_patches(key, part):
    owners = layout(key)[0]
    row_owner = jnp.repeat(owners, TILE)
    base = jax.random.truncated_normal(jax.random.fold_in(key, 111), -4.0, 4.0, (D,))
    region = jax.random.truncated_normal(jax.random.fold_in(key, 112), -4.0, 4.0, (N_DP, D))
    noise = jax.random.truncated_normal(jax.random.fold_in(key, 113), -4.0, 4.0, (ROWS, D))
    rows = base[None, :] + 0.7 * region[row_owner] + noise
    return rows.astype(jnp.bfloat16)


def query_key(key):
    first_draw = jax.random.truncated_normal(jax.random.fold_in(key, 201), -4.0, 4.0, (D, D)) / math.sqrt(D)
    second_draw = jax.random.truncated_normal(jax.random.fold_in(key, 202), -4.0, 4.0, (D, D)) / math.sqrt(D)
    return (first_draw, second_draw)


def draw_w_query(key, part):
    first_draw, second_draw = query_key(key)
    return first_draw.astype(jnp.bfloat16)


def draw_w_key(key, part):
    first_draw, second_draw = query_key(key)
    return second_draw.astype(jnp.bfloat16)


def level_of(rng, extent, pieces, low, high):
    level, own = 1.0, jax.random.fold_in(rng, 6)
    for dim, parts in pieces:
        steps = jnp.exp(jax.random.uniform(jax.random.fold_in(own, dim), (parts,), jnp.float32, low / len(pieces), high / len(pieces)))
        level = level * jnp.repeat(steps, extent[dim] // parts).reshape([-1 if axis == dim else 1 for axis in range(len(extent))])
    return level


def bell_draw(stream_key, dims, deviation, most, cuts=(), kind=jnp.bfloat16):
    entries = deviation * jax.random.normal(stream_key, dims, jnp.float32)
    if cuts:
        entries = entries * level_of(stream_key, dims, cuts, -0.22, 0.18)
    return jnp.clip(entries, -most, most).astype(kind)


def setup_inputs(seed: int = 0) -> dict:
    streams_of = jax.random.split(jax.random.key(seed), 9)
    return {
        "patches": draw_patches(jax.random.fold_in(streams_of[8], 71), 0),
        "dest_owner": draw_dest_owner(jax.random.fold_in(streams_of[8], 71), 0),
        "dest_slot": draw_dest_slot(jax.random.fold_in(streams_of[8], 71), 0),
        "packed_image": draw_packed_image(jax.random.fold_in(streams_of[8], 71), 0),
        "w_query": draw_w_query(jax.random.fold_in(streams_of[8], 71), 0),
        "w_key": draw_w_key(jax.random.fold_in(streams_of[8], 71), 0),
        "w_value": bell_draw(streams_of[6], (D, D), D ** -0.5, 0.1875, ((1, 4),)),
        "w_out": bell_draw(streams_of[7], (D, D), D ** -0.5, 0.1875, ((0, 4),)),
    }


EPSILON = 1e-06

def normalize(rows):
    values = rows.astype(jnp.float32)
    centred = values - lax.optimization_barrier(jnp.mean(values, axis=-1, keepdims=True))
    spread = lax.optimization_barrier(jnp.mean(centred * centred, axis=-1, keepdims=True))
    return (centred * lax.rsqrt(spread + EPSILON)).astype(jnp.bfloat16)

def attend(queries, key_rows, values, allowed, present):
    scores = jnp.einsum('qhd,khd->hqk', queries.astype(jnp.float32), key_rows.astype(jnp.float32)) * HEAD_DIM ** (-0.5)
    masked = jnp.where(allowed[None], scores, -1e+30)
    peak = lax.optimization_barrier(jnp.max(masked, axis=-1, keepdims=True))
    raised = jnp.where(allowed[None], jnp.exp(scores - peak), 0.0)
    denominator = lax.optimization_barrier(jnp.sum(raised, axis=-1, keepdims=True))
    denominator = jnp.where(present[None, :, None], denominator, 1.0)
    weights = (raised / denominator).astype(jnp.bfloat16)
    return jnp.einsum('hqk,khd->qhd', weights.astype(jnp.float32), values.astype(jnp.float32)).astype(jnp.bfloat16)

def reference(patches, dest_owner, dest_slot, packed_image, w_query, w_key, w_value, w_out):
    seq_rows = SLOTS * TILE
    target = dest_owner * SLOTS + dest_slot
    source_of = jnp.argsort(target).astype(jnp.int32)
    packed = jnp.take(patches.reshape(N_DP * SLOTS, TILE, D), source_of, axis=0).reshape(N_DP, seq_rows, D)
    segment_ids = packed_image.reshape(N_DP, SLOTS)
    labels = jnp.arange(IMG_OWN, dtype=jnp.int32)

    def owner_block(inputs):
        rows, seg_tiles = inputs
        segment = jnp.repeat(seg_tiles, TILE)
        present = segment >= 0
        normed = normalize(rows)
        queries = jnp.dot(normed, w_query, preferred_element_type=jnp.float32).astype(jnp.bfloat16)
        key_rows = jnp.dot(normed, w_key, preferred_element_type=jnp.float32).astype(jnp.bfloat16)
        values = jnp.dot(normed, w_value, preferred_element_type=jnp.float32).astype(jnp.bfloat16)
        queries = queries.reshape(seq_rows, HEADS, HEAD_DIM)
        key_rows = key_rows.reshape(seq_rows, HEADS, HEAD_DIM)
        values = values.reshape(seq_rows, HEADS, HEAD_DIM)
        allowed = (segment[:, None] == segment[None, :]) & present[:, None]
        attended = attend(queries, key_rows, values, allowed, present).reshape(seq_rows, D)
        groups = attended.reshape(seq_rows, N_MP, D // N_MP).astype(jnp.float32)
        out_groups = w_out.reshape(N_MP, D // N_MP, D).astype(jnp.float32)
        head_term = jnp.einsum('rgc,gcd->grd', groups, out_groups)
        rounded = lax.optimization_barrier(head_term.astype(jnp.bfloat16)).astype(jnp.float32)
        projected = lax.optimization_barrier(jnp.sum(rounded, axis=0))
        result_rows = jnp.where(present[:, None], rows.astype(jnp.float32) + projected, 0.0)
        member = (segment[None, :] == labels[:, None]).astype(jnp.float32)
        sums = jnp.dot(member, result_rows, precision=lax.Precision.HIGHEST)
        image_rows = lax.optimization_barrier(jnp.sum(member, axis=1))
        filled = image_rows > 0
        pooled = sums / jnp.maximum(image_rows, 1.0)[:, None]
        local_sum = lax.optimization_barrier(jnp.sum(jnp.where(filled[:, None], pooled, 0.0), axis=0))
        local_count = jnp.sum(filled.astype(jnp.float32))
        return (result_rows.astype(jnp.bfloat16), pooled, filled, local_sum, local_count)
    out_rows, pooled, filled, local_sum, local_count = lax.map(owner_block, (packed, segment_ids))
    centre = lax.optimization_barrier(jnp.sum(local_sum, axis=0)) / jnp.sum(local_count)
    pooled_out = jnp.where(filled[:, :, None], pooled - centre[None, None, :], 0.0).astype(jnp.bfloat16)
    return (out_rows.reshape(N_DP * seq_rows, D), pooled_out.reshape(N_DP * IMG_OWN, D))
```

```python
import functools

import jax
import jax.numpy as jnp
from jax import lax
from jax.experimental import pallas as pl
from jax.experimental.pallas import tpu as pltpu
from jax.sharding import PartitionSpec as P

HEAD_DIM = 64
IMG_OWN = 16
EPSILON = 1e-06
MAX_TILES = 16
Q_TILES = 8

VMEM = pl.BlockSpec(memory_space=pltpu.VMEM)
SMEM = pl.BlockSpec(memory_space=pltpu.SMEM)
LIMIT = 60 * 1024 * 1024


def rows_of(index, size):
    return pl.ds(pl.multiple_of(index * size, size), size)


def pack_kernel(
    senders, tile, column, owner, slot, image, patches, outgoing, meta, table, count, first, last
):
    slots = image.shape[0]
    per_owner = slots // senders
    del column

    def clear(index, carry):
        count[index] = 0
        return carry

    lax.fori_loop(0, senders, clear, 0)

    def place(index, carry):
        target = owner[index]
        rank = count[target]
        count[target] = rank + 1
        meta[target * 8, rank] = slot[index]
        outgoing[rows_of(target * per_owner + rank, tile), :] = patches[rows_of(index, tile), :]
        return carry

    lax.fori_loop(0, slots, place, 0, unroll=4)

    def forward(index, start):
        before = image[jnp.maximum(index - 1, 0)]
        start = jnp.where(image[index] == before, start, index)
        first[index] = start
        return start

    lax.fori_loop(0, slots, forward, 0)

    def backward(step, end):
        index = slots - 1 - step
        after = image[jnp.minimum(index + 1, slots - 1)]
        end = jnp.where(image[index] == after, end, index + 1)
        last[index] = end
        return end

    lax.fori_loop(0, slots, backward, slots)

    def block(index, carry):
        split = last[index * Q_TILES]
        clipped = jnp.minimum(split, slots - 1)
        begin = first[index * Q_TILES] * tile
        table[0, index] = begin
        table[1, index] = split * tile
        table[2, index] = jnp.where(image[clipped] >= 0, last[clipped], split) * tile
        return carry

    lax.fori_loop(0, slots // Q_TILES, block, 0)
    final = last[slots - 1]
    dead = image[slots - 1] < 0
    table[4, 0] = jnp.where(dead, first[slots - 1], final) * tile


def pack(owner, slot, image, patches, senders, splits):
    slots = owner.shape[0]
    rows, width = patches.shape
    part = width // splits
    tile = rows // slots
    column = lax.axis_index("mp").astype(jnp.int32).reshape(1)
    grid_spec = pltpu.PrefetchScalarGridSpec(
        num_scalar_prefetch=1,
        grid=(1,),
        in_specs=[SMEM, SMEM, SMEM, pl.BlockSpec((rows, part), lambda i, col: (0, col[0]))],
        out_specs=[
            pl.BlockSpec((rows, part), lambda i, col: (0, 0)),
            SMEM,
            SMEM,
        ],
        scratch_shapes=[
            pltpu.SMEM((senders,), jnp.int32),
            pltpu.SMEM((slots,), jnp.int32),
            pltpu.SMEM((slots,), jnp.int32),
        ],
    )
    return pl.pallas_call(
        functools.partial(pack_kernel, senders, tile),
        out_shape=[
            jax.ShapeDtypeStruct((rows, part), patches.dtype),
            jax.ShapeDtypeStruct((senders * 8, 128), jnp.int32),
            jax.ShapeDtypeStruct((8, 128), jnp.int32),
        ],
        grid_spec=grid_spec,
        name="pack",
    )(column, owner, slot, image, patches)


def partners(splits):
    mine = lax.axis_index("mp")
    sibling = mine + 1 - 2 * lax.rem(mine, 2)
    across = lax.rem(mine + splits // 2, splits)
    return mine, sibling, across


def greet(senders, sibling, across, all_mp=None):
    owner = lax.axis_index("dp")
    barrier = pltpu.get_barrier_semaphore()

    def one(step, carry):
        pl.semaphore_signal(barrier, inc=1, device_id={"dp": lax.rem(owner + step, senders)})
        return carry

    lax.fori_loop(1, senders, one, 0)
    peers = (sibling, across) if all_mp is None else all_mp
    for peer in peers:
        pl.semaphore_signal(barrier, inc=1, device_id={"mp": peer})
    pl.semaphore_wait(barrier, senders - 1 + len(peers))


def exchange_kernel(
    senders, splits, outgoing, meta, gathered, slots_in,
    meta_send, meta_recv, send, recv, sib_send, sib_recv, far_send, far_recv, fwd_send, fwd_recv,
    local_sem,
):
    owner = lax.axis_index("dp")
    mine, sibling, across = partners(splits)
    block = outgoing.shape[0] // senders
    greet(senders, sibling, across)

    def meta_copy(target, source):
        return pltpu.make_async_remote_copy(
            src_ref=meta.at[rows_of(target, 8), :],
            dst_ref=slots_in.at[rows_of(source, 8), :],
            send_sem=meta_send.at[target],
            recv_sem=meta_recv.at[source],
            device_id={"dp": target},
        )

    def data_copy(target, source):
        return pltpu.make_async_remote_copy(
            src_ref=outgoing.at[rows_of(target, block), :],
            dst_ref=gathered.at[mine, rows_of(source, block), :],
            send_sem=send.at[target],
            recv_sem=recv.at[source],
            device_id={"dp": target},
        )

    def share(part, source, peer, send_sem, recv_sem):
        view = gathered.at[part, rows_of(source, block), :]
        return pltpu.make_async_remote_copy(
            src_ref=view,
            dst_ref=view,
            send_sem=send_sem.at[source],
            recv_sem=recv_sem.at[source],
            device_id={"mp": peer},
        )

    def start_all(step, carry):
        target = lax.rem(owner + step, senders)
        data_copy(target, owner).start()
        meta_copy(target, owner).start()
        return carry

    lax.fori_loop(1, senders, start_all, 0)
    own = pltpu.make_async_copy(
        outgoing.at[rows_of(owner, block), :],
        gathered.at[mine, rows_of(owner, block), :],
        local_sem.at[0],
    )
    own.start()
    own_meta = pltpu.make_async_copy(
        meta.at[rows_of(owner, 8), :], slots_in.at[rows_of(owner, 8), :], local_sem.at[1]
    )
    own_meta.start()
    own.wait()
    own_meta.wait()

    def spread(source):
        share(mine, source, across, far_send, far_recv).start()
        share(mine, source, sibling, sib_send, sib_recv).start()

    def relay(source):
        share(across, source, across, far_send, far_recv).wait_recv()
        share(across, source, sibling, fwd_send, fwd_recv).start()

    spread(owner)

    def arrive(step, carry):
        source = lax.rem(owner + senders - step, senders)
        data_copy(owner, source).wait_recv()
        spread(source)

        relay(lax.rem(owner + senders - step + 1, senders))
        return carry

    lax.fori_loop(1, senders, arrive, 0)
    relay(lax.rem(owner + 1, senders))
    other = lax.rem(sibling + splits // 2, splits)

    def finish(step, carry):
        source = lax.rem(owner + senders - step, senders)
        share(sibling, source, sibling, sib_send, sib_recv).wait_recv()
        share(other, source, sibling, fwd_send, fwd_recv).wait_recv()
        share(mine, source, across, far_send, far_recv).wait_send()
        share(mine, source, sibling, sib_send, sib_recv).wait_send()
        share(across, source, sibling, fwd_send, fwd_recv).wait_send()
        return carry

    lax.fori_loop(0, senders, finish, 0)

    def finish_peers(step, carry):
        source = lax.rem(owner + senders - step, senders)
        target = lax.rem(owner + step, senders)
        meta_copy(owner, source).wait_recv()
        meta_copy(target, owner).wait_send()
        data_copy(target, owner).wait_send()
        return carry

    lax.fori_loop(1, senders, finish_peers, 0)


def exchange(outgoing, meta, senders, splits):
    rows, part = outgoing.shape
    return pl.pallas_call(
        functools.partial(exchange_kernel, senders, splits),
        out_shape=[
            jax.ShapeDtypeStruct((splits, rows, part), outgoing.dtype),
            jax.ShapeDtypeStruct(meta.shape, meta.dtype),
        ],
        in_specs=[VMEM, VMEM],
        out_specs=[VMEM, VMEM],
        scratch_shapes=[pltpu.SemaphoreType.DMA((senders,))] * 10 + [pltpu.SemaphoreType.DMA((2,))],
        compiler_params=pltpu.CompilerParams(
            collective_id=0, has_side_effects=True, vmem_limit_bytes=LIMIT
        ),
        name="exchange",
    )(outgoing, meta)


def project_kernel(
    senders, tile, slots_in, gathered, w_query, w_key, w_value,
    q_out, k_out, v_out, own_out, arrived, rows_buf,
):
    splits, rows, part = gathered.shape
    slots = rows // tile
    per_owner = slots // senders
    width = splits * part
    mine = lax.axis_index("mp")
    pairs = part // 128
    q_rows = Q_TILES * tile
    chunk = rows_buf.shape[0]
    chunk_tiles = chunk // tile

    def note(index, carry):
        source = index // per_owner
        arrived[slots_in[source * 8, index - source * per_owner]] = index
        return carry

    lax.fori_loop(0, slots, note, 0, unroll=4)

    def step(index, carry):
        for t in range(chunk_tiles):
            place = arrived[index * chunk_tiles + t]
            for p in range(splits):
                rows_buf[t * tile : (t + 1) * tile, p * part : (p + 1) * part] = gathered[
                    p, rows_of(place, tile), :
                ]
            own_out[rows_of(index * chunk_tiles + t, tile), :] = gathered[
                mine, rows_of(place, tile), :
            ]
        values = rows_buf[...].astype(jnp.float32)
        centred = values - jnp.sum(values, axis=-1, keepdims=True) * (1.0 / width)
        spread = jnp.sum(centred * centred, axis=-1, keepdims=True) * (1.0 / width)
        normed = (centred * lax.rsqrt(spread + EPSILON)).astype(jnp.bfloat16)
        here = rows_of(index, chunk)
        query = jnp.dot(normed, w_query[...], preferred_element_type=jnp.float32)
        query = query.astype(jnp.bfloat16)
        low = lax.broadcasted_iota(jnp.int32, (q_rows, 128), 1) < HEAD_DIM
        for b in range(chunk // q_rows):
            for p in range(pairs):
                pair = query[b * q_rows : (b + 1) * q_rows, p * 128 : (p + 1) * 128]
                zero = jnp.zeros_like(pair)
                base = (index * (chunk // q_rows) + b) * 2
                q_out[p, rows_of(base, q_rows), :] = jnp.where(low, pair, zero)
                q_out[p, rows_of(base + 1, q_rows), :] = jnp.where(low, zero, pair)
        k_out[here, :] = jnp.dot(normed, w_key[...], preferred_element_type=jnp.float32).astype(
            jnp.bfloat16
        )
        value = jnp.dot(normed, w_value[...], preferred_element_type=jnp.float32).astype(
            jnp.bfloat16
        )
        for p in range(pairs):
            v_out[here, p * 256 : p * 256 + 128] = value[:, p * 128 : (p + 1) * 128]
            v_out[here, p * 256 + 128 : (p + 1) * 256] = jnp.ones((chunk, 128), jnp.bfloat16)
        return carry

    lax.fori_loop(0, rows // chunk, step, 0)


def project(gathered, slots_in, w_query, w_key, w_value, senders, tile):
    splits, rows, part = gathered.shape
    pairs = part // 128
    chunk = 2 * Q_TILES * tile
    kind = gathered.dtype
    return pl.pallas_call(
        functools.partial(project_kernel, senders, tile),
        out_shape=[
            jax.ShapeDtypeStruct((pairs, 2 * rows, 128), kind),
            jax.ShapeDtypeStruct((rows, part), kind),
            jax.ShapeDtypeStruct((rows, 2 * part), kind),
            jax.ShapeDtypeStruct((rows, part), kind),
        ],
        in_specs=[SMEM, VMEM, VMEM, VMEM, VMEM],
        out_specs=[VMEM, VMEM, VMEM, VMEM],
        scratch_shapes=[
            pltpu.SMEM((rows // tile,), jnp.int32),
            pltpu.VMEM((chunk, splits * part), kind),
        ],
        compiler_params=pltpu.CompilerParams(vmem_limit_bytes=LIMIT),
        name="project",
    )(slots_in, gathered, w_query, w_key, w_value)


def attend_kernel(
    senders, splits, tile, table, q_ref, k_ref, v_ref, own, w_out, image, out, pooled_out,
    att, w_cols, tile_sums, message, inbox,
    w_send, w_recv, sib_send, sib_recv, far_send, far_recv, fwd_send, fwd_recv, sum_send, sum_recv,
    local_sem,
):
    owner = lax.axis_index("dp")
    mine, sibling, across = partners(splits)
    other = lax.rem(sibling + splits // 2, splits)
    rows, part = k_ref.shape
    q_rows = Q_TILES * tile
    window = q_rows + 2 * MAX_TILES * tile
    chunk = 2 * q_rows
    chunks = rows // chunk
    pairs = part // 128
    others = [lax.rem(mine + step, splits) for step in range(1, splits)]
    greet(senders, sibling, across, others)

    def weight_copy(target, source):
        return pltpu.make_async_remote_copy(
            src_ref=w_out.at[:, pl.ds(pl.multiple_of(target * part, part), part)],
            dst_ref=w_cols.at[source],
            send_sem=w_send.at[target],
            recv_sem=w_recv.at[source],
            device_id={"mp": target},
        )

    for target in others:
        weight_copy(target, mine).start()
    own_w = pltpu.make_async_copy(
        w_out.at[:, pl.ds(pl.multiple_of(mine * part, part), part)], w_cols.at[mine], local_sem.at[0]
    )
    own_w.start()

    def share(group, index, peer, send_sem, recv_sem):
        view = att.at[group, rows_of(index, chunk), :]
        return pltpu.make_async_remote_copy(
            src_ref=view,
            dst_ref=view,
            send_sem=send_sem.at[index],
            recv_sem=recv_sem.at[index],
            device_id={"mp": peer},
        )

    def spread(index):
        share(mine, index, across, far_send, far_recv).start()
        share(mine, index, sibling, sib_send, sib_recv).start()

    def relay(index):
        share(across, index, across, far_send, far_recv).wait_recv()
        share(across, index, sibling, fwd_send, fwd_recv).start()

    low = lax.broadcasted_iota(jnp.int32, (q_rows, 128), 1) < HEAD_DIM

    def attend(block):
        begin, split, end = (table[i, block] for i in range(3))
        start = jnp.clip(block * q_rows - MAX_TILES * tile, 0, rows - window)
        row = lax.broadcasted_iota(jnp.int32, (q_rows, 1), 0) + block * q_rows
        column = lax.broadcasted_iota(jnp.int32, (q_rows, window), 1) + start
        lowest = jnp.where(row < split, begin, split)
        highest = jnp.where(row < split, split, end)
        allowed = (column >= lowest) & (column < highest)
        bias = jnp.where(allowed, 0.0, -1e30)
        keys = pl.ds(pl.multiple_of(start, q_rows), window)
        for p in range(pairs):
            queries = q_ref[p, rows_of(block, 2 * q_rows), :]
            key_rows = k_ref[keys, p * 128 : (p + 1) * 128]
            values = v_ref[keys, p * 256 : (p + 1) * 256]
            scores = lax.dot_general(
                queries, key_rows, (((1,), (1,)), ((), ())), preferred_element_type=jnp.float32
            )
            halves = []
            for half in range(2):
                masked = scores[half * q_rows : (half + 1) * q_rows, :] * HEAD_DIM**-0.5 + bias
                peak = jnp.max(masked, axis=-1, keepdims=True)
                raised = jnp.exp(masked - peak).astype(jnp.bfloat16)
                mixed = jnp.dot(raised, values, preferred_element_type=jnp.float32)
                halves.append(mixed[:, :128] / mixed[:, 128:])
            att[mine, rows_of(block, q_rows), p * 128 : (p + 1) * 128] = jnp.where(
                low, halves[0], halves[1]
            ).astype(jnp.bfloat16)

    def attention_step(index, carry):
        attend(2 * index)

        @pl.when(index >= 1)
        def _():
            spread(index - 1)

        attend(2 * index + 1)

        @pl.when(index >= 4)
        def _():
            relay(index - 4)

        return carry

    lax.fori_loop(0, chunks, attention_step, 0)
    own_w.wait()
    for source in others:
        weight_copy(mine, source).wait_recv()
    spread(chunks - 1)
    live = table[4, 0]
    lag = min(4, chunks)

    def output_step(index, carry):
        @pl.when(index < lag)
        def _():
            relay(chunks - lag + index)

        share(sibling, index, sibling, sib_send, sib_recv).wait_recv()
        share(other, index, sibling, fwd_send, fwd_recv).wait_recv()
        here = rows_of(index, chunk)
        total = jnp.zeros((chunk, part), jnp.float32)
        for group in range(splits):
            term = jnp.dot(att[group, here, :], w_cols[group], preferred_element_type=jnp.float32)
            total = total + term.astype(jnp.bfloat16).astype(jnp.float32)
        row = lax.broadcasted_iota(jnp.int32, (chunk, 1), 0) + index * chunk
        result = jnp.where(row < live, own[here, :].astype(jnp.float32) + total, 0.0)
        out[here, :] = result.astype(jnp.bfloat16)
        tile_sums[rows_of(index, chunk // tile), :] = jnp.sum(
            result.reshape(chunk // tile, tile, part), axis=1
        )
        return carry

    lax.fori_loop(0, chunks, output_step, 0)

    slots = rows // tile
    labels = lax.broadcasted_iota(jnp.int32, (IMG_OWN, slots), 0)
    member = (image[...] == labels).astype(jnp.float32)
    sums = jnp.dot(
        member, tile_sums[...], precision=lax.Precision.HIGHEST, preferred_element_type=jnp.float32
    )
    image_rows = jnp.sum(member, axis=1, keepdims=True) * float(tile)
    filled = image_rows > 0
    pooled = sums / jnp.maximum(image_rows, 1.0)
    local_sum = jnp.sum(jnp.where(filled, pooled, 0.0), axis=0, keepdims=True)
    local_count = jnp.sum(filled.astype(jnp.float32), axis=0, keepdims=True)
    message[:, :part] = jnp.broadcast_to(local_sum, (8, part))
    message[:, part:] = jnp.broadcast_to(local_count, (8, 128))

    def drain(index, carry):
        share(mine, index, across, far_send, far_recv).wait_send()
        share(mine, index, sibling, sib_send, sib_recv).wait_send()
        share(across, index, sibling, fwd_send, fwd_recv).wait_send()
        return carry

    lax.fori_loop(0, chunks, drain, 0)
    for target in others:
        weight_copy(target, mine).wait_send()

    def sum_copy(target, source):
        return pltpu.make_async_remote_copy(
            src_ref=message,
            dst_ref=inbox.at[source],
            send_sem=sum_send.at[target],
            recv_sem=sum_recv.at[source],
            device_id={"dp": target},
        )

    def send_sum(step, carry):
        sum_copy(lax.rem(owner + step, senders), owner).start()
        return carry

    lax.fori_loop(1, senders, send_sum, 0)
    inbox[owner] = message[...]

    def wait_sum(step, carry):
        sum_copy(owner, lax.rem(owner + senders - step, senders)).wait_recv()
        sum_copy(lax.rem(owner + step, senders), owner).wait_send()
        return carry

    lax.fori_loop(1, senders, wait_sum, 0)
    grand = lax.fori_loop(
        0, senders, lambda i, acc: acc + inbox[i], jnp.zeros(message.shape, jnp.float32)
    )
    centre = grand[0:1, :part] / grand[0:1, part : part + 1]
    pooled_out[...] = jnp.where(filled, pooled - centre, 0.0).astype(jnp.bfloat16)


def finish_block(table, queries, keys, values, own, w_out, image, senders, splits, tile):
    rows, part = keys.shape
    chunks = rows // (2 * Q_TILES * tile)
    dma = pltpu.SemaphoreType.DMA
    return pl.pallas_call(
        functools.partial(attend_kernel, senders, splits, tile),
        out_shape=[
            jax.ShapeDtypeStruct((rows, part), keys.dtype),
            jax.ShapeDtypeStruct((IMG_OWN, part), keys.dtype),
        ],
        in_specs=[SMEM] + [VMEM] * 6,
        out_specs=[VMEM, VMEM],
        scratch_shapes=[
            pltpu.VMEM((splits, rows, part), keys.dtype),
            pltpu.VMEM((splits, part, part), keys.dtype),
            pltpu.VMEM((rows // tile, part), jnp.float32),
            pltpu.VMEM((8, part + 128), jnp.float32),
            pltpu.VMEM((senders, 8, part + 128), jnp.float32),
            dma((splits,)),
            dma((splits,)),
        ]
        + [dma((chunks,))] * 6
        + [dma((senders,))] * 2
        + [dma((1,))],
        compiler_params=pltpu.CompilerParams(
            collective_id=1, has_side_effects=True, vmem_limit_bytes=LIMIT
        ),
        name="attend",
    )(table, queries, keys, values, own, w_out, image)


def on_device(patches, dest_owner, dest_slot, packed_image, w_query, w_key, w_value, w_out):
    senders = lax.axis_size("dp")
    splits = lax.axis_size("mp")
    tile = patches.shape[0] // dest_owner.shape[0]
    outgoing, meta, table = pack(dest_owner, dest_slot, packed_image, patches, senders, splits)
    gathered, slots_in = exchange(outgoing, meta, senders, splits)
    queries, keys, values, own = project(
        gathered, slots_in, w_query, w_key, w_value, senders, tile
    )
    packed_out, pooled_out = finish_block(
        table, queries, keys, values, own, w_out, packed_image[None, :], senders, splits, tile
    )
    return (packed_out, pooled_out)


def solution(mesh):
    in_specs = (
        P("dp", None),
        P("dp"),
        P("dp"),
        P("dp"),
        P(None, "mp"),
        P(None, "mp"),
        P(None, "mp"),
        P("mp", None),
    )
    out_specs = (P("dp", "mp"), P("dp", "mp"))
    return jax.shard_map(
        on_device, mesh=mesh, in_specs=in_specs, out_specs=out_specs, check_vma=False
    )
```

```python
import functools

import jax
import jax.numpy as jnp
from jax import lax
from jax.experimental import pallas as pl
from jax.experimental.pallas import tpu as pltpu
from jax.sharding import PartitionSpec as P

HEAD_DIM = 64
IMG_OWN = 16
EPSILON = 1e-06
MAX_TILES = 16
Q_TILES = 8

VMEM = pl.BlockSpec(memory_space=pltpu.VMEM)
SMEM = pl.BlockSpec(memory_space=pltpu.SMEM)
LIMIT = 60 * 1024 * 1024


def rows_of(index, size):
    return pl.ds(pl.multiple_of(index * size, size), size)


def pack_kernel(
    senders, tile, scalars, owner, slot, part_rows, patches, outgoing, meta, kept, count, kept_sem
):
    slots = owner.shape[0]
    per_owner = slots // senders
    mine = scalars[1]

    def clear(index, carry):
        count[index] = 0
        return carry

    lax.fori_loop(0, senders, clear, 0)

    def keep(source, target):
        return pltpu.make_async_copy(
            patches.at[rows_of(source, tile), :], kept.at[rows_of(target, tile), :], kept_sem.at[target]
        )

    def place(index, carry):
        target = owner[index]
        rank = count[target]
        count[target] = rank + 1
        meta[target * 8, rank] = slot[index]
        outgoing[rows_of(target * per_owner + rank, tile), :] = part_rows[rows_of(index, tile), :]

        @pl.when(target == mine)
        def _():
            keep(index, rank).start()

        return carry

    lax.fori_loop(0, slots, place, 0, unroll=4)

    def settle(index, carry):
        keep(index, index).wait()
        return carry

    lax.fori_loop(0, per_owner, settle, 0)


def pack(owner, slot, patches, senders, splits):
    slots = owner.shape[0]
    rows, width = patches.shape
    part = width // splits
    tile = rows // slots
    block = rows // senders
    scalars = jnp.stack([lax.axis_index("mp"), lax.axis_index("dp")]).astype(jnp.int32)
    grid_spec = pltpu.PrefetchScalarGridSpec(
        num_scalar_prefetch=1,
        grid=(1,),
        in_specs=[
            SMEM,
            SMEM,
            pl.BlockSpec((rows, part), lambda i, col: (0, col[0])),
            pl.BlockSpec(memory_space=pl.ANY),
        ],
        out_specs=[
            pl.BlockSpec((rows, part), lambda i, col: (0, 0)),
            SMEM,
            VMEM,
        ],
        scratch_shapes=[pltpu.SMEM((senders,), jnp.int32), pltpu.SemaphoreType.DMA((slots // senders,))],
    )
    return pl.pallas_call(
        functools.partial(pack_kernel, senders, tile),
        out_shape=[
            jax.ShapeDtypeStruct((rows, part), patches.dtype),
            jax.ShapeDtypeStruct((senders * 8, 128), jnp.int32),
            jax.ShapeDtypeStruct((block, width), patches.dtype),
        ],
        grid_spec=grid_spec,
        name="pack",
    )(scalars, owner, slot, patches, patches)


def index_kernel(per_owner, slots_in, arrived):
    def note(index, carry):
        source = index // per_owner
        arrived[slots_in[source * 8, index - source * per_owner]] = index
        return carry

    lax.fori_loop(0, arrived.shape[0], note, 0, unroll=8)


def arrival(slots_in, slots, senders):
    return pl.pallas_call(
        functools.partial(index_kernel, slots // senders),
        out_shape=jax.ShapeDtypeStruct((slots,), jnp.int32),
        in_specs=[SMEM],
        out_specs=SMEM,
        name="arrival",
    )(slots_in)


def partners(splits):
    mine = lax.axis_index("mp")
    sibling = mine + 1 - 2 * lax.rem(mine, 2)
    across = lax.rem(mine + splits // 2, splits)
    return mine, sibling, across


def greet(senders, peers):
    owner = lax.axis_index("dp")
    barrier = pltpu.get_barrier_semaphore()

    def one(step, carry):
        pl.semaphore_signal(barrier, inc=1, device_id={"dp": lax.rem(owner + step, senders)})
        return carry

    lax.fori_loop(1, senders, one, 0)
    for peer in peers:
        pl.semaphore_signal(barrier, inc=1, device_id={"mp": peer})
    pl.semaphore_wait(barrier, senders - 1 + len(peers))


def exchange_kernel(
    senders, splits, tile, outgoing, meta, kept, w_query, w_key, w_value, w_out,
    q_out, k_out, v_out, own_out, slots_in, w_cols, gathered, w_send, w_recv, meta_send, meta_recv, send, recv, sib_send, sib_recv, far_send, far_recv, fwd_send, fwd_recv,
    local_sem,
):
    owner = lax.axis_index("dp")
    mine, sibling, across = partners(splits)
    rows, part = outgoing.shape
    block = rows // senders
    width = splits * part
    block_tiles = block // tile
    others = [lax.rem(mine + step, splits) for step in range(1, splits)]
    greet(senders, others)

    def meta_copy(target, source):
        return pltpu.make_async_remote_copy(
            src_ref=meta.at[rows_of(target, 8), :],
            dst_ref=slots_in.at[rows_of(source, 8), :],
            send_sem=meta_send.at[target],
            recv_sem=meta_recv.at[source],
            device_id={"dp": target},
        )

    def data_copy(target, source):
        return pltpu.make_async_remote_copy(
            src_ref=outgoing.at[rows_of(target, block), :],
            dst_ref=gathered.at[mine, rows_of(source, block), :],
            send_sem=send.at[target],
            recv_sem=recv.at[source],
            device_id={"dp": target},
        )

    def share(part, source, peer, send_sem, recv_sem):
        view = gathered.at[part, rows_of(source, block), :]
        return pltpu.make_async_remote_copy(
            src_ref=view,
            dst_ref=view,
            send_sem=send_sem.at[source],
            recv_sem=recv_sem.at[source],
            device_id={"mp": peer},
        )

    def weight_copy(target, source):
        return pltpu.make_async_remote_copy(
            src_ref=w_out.at[:, pl.ds(pl.multiple_of(target * part, part), part)],
            dst_ref=w_cols.at[source],
            send_sem=w_send.at[target],
            recv_sem=w_recv.at[source],
            device_id={"mp": target},
        )

    def start_all(step, carry):
        target = lax.rem(owner + step, senders)
        data_copy(target, owner).start()
        meta_copy(target, owner).start()
        return carry

    lax.fori_loop(1, senders, start_all, 0)
    for target in others:
        weight_copy(target, mine).start()
    own_w = pltpu.make_async_copy(
        w_out.at[:, pl.ds(pl.multiple_of(mine * part, part), part)], w_cols.at[mine], local_sem.at[0]
    )
    own_w.start()
    own_meta = pltpu.make_async_copy(
        meta.at[rows_of(owner, 8), :], slots_in.at[rows_of(owner, 8), :], local_sem.at[1]
    )
    own_meta.start()

    def project(parts, source):
        values = jnp.concatenate(parts, axis=1).astype(jnp.float32)
        centred = values - jnp.sum(values, axis=-1, keepdims=True) * (1.0 / width)
        spread_of = jnp.sum(centred * centred, axis=-1, keepdims=True) * (1.0 / width)
        normed = (centred * lax.rsqrt(spread_of + EPSILON)).astype(jnp.bfloat16)
        here = pl.ds(source * block_tiles, block_tiles)
        for weight, result in ((w_query, q_out), (w_key, k_out), (w_value, v_out)):
            product = jnp.dot(normed, weight[...], preferred_element_type=jnp.float32)
            result[here] = product.astype(jnp.bfloat16).reshape(block_tiles, tile, part)

    def spread(source):
        share(mine, source, across, far_send, far_recv).start()
        share(mine, source, sibling, sib_send, sib_recv).start()

    def relay(source):
        share(across, source, across, far_send, far_recv).wait_recv()
        share(across, source, sibling, fwd_send, fwd_recv).start()

    other = lax.rem(sibling + splits // 2, splits)

    def source_at(step):
        return lax.rem(owner + senders - step, senders)

    def compute(source):
        share(sibling, source, sibling, sib_send, sib_recv).wait_recv()
        share(other, source, sibling, fwd_send, fwd_recv).wait_recv()
        here = rows_of(source, block)
        project([gathered[p, here, :] for p in range(splits)], source)
        own_out[pl.ds(source * block_tiles, block_tiles)] = gathered[mine, here, :].reshape(
            block_tiles, tile, part
        )

    project([kept[...]], owner)
    own_out[pl.ds(owner * block_tiles, block_tiles)] = outgoing[rows_of(owner, block), :].reshape(
        block_tiles, tile, part
    )

    def arrive(step, carry):
        source = source_at(step)
        data_copy(owner, source).wait_recv()
        spread(source)

        @pl.when(step >= 2)
        def _():
            relay(source_at(step - 1))

        @pl.when(step >= 3)
        def _():
            compute(source_at(step - 2))

        return carry

    lax.fori_loop(1, senders, arrive, 0)
    relay(source_at(senders - 1))

    def compute_rest(step, carry):
        compute(source_at(step))
        return carry

    lax.fori_loop(max(1, senders - 2), senders, compute_rest, 0)
    own_w.wait()
    own_meta.wait()
    for target in others:
        weight_copy(mine, target).wait_recv()
        weight_copy(target, mine).wait_send()

    def finish(step, carry):
        source = source_at(step)
        share(mine, source, across, far_send, far_recv).wait_send()
        share(mine, source, sibling, sib_send, sib_recv).wait_send()
        share(across, source, sibling, fwd_send, fwd_recv).wait_send()
        return carry

    lax.fori_loop(1, senders, finish, 0)

    def finish_peers(step, carry):
        source = lax.rem(owner + senders - step, senders)
        target = lax.rem(owner + step, senders)
        meta_copy(owner, source).wait_recv()
        meta_copy(target, owner).wait_send()
        data_copy(target, owner).wait_send()
        return carry

    lax.fori_loop(1, senders, finish_peers, 0)


def exchange(outgoing, meta, kept, w_query, w_key, w_value, w_out, senders, splits, tile):
    rows, part = outgoing.shape
    kind = outgoing.dtype
    dma = pltpu.SemaphoreType.DMA
    tiles = jax.ShapeDtypeStruct((rows // tile, tile, part), kind)
    return pl.pallas_call(
        functools.partial(exchange_kernel, senders, splits, tile),
        out_shape=[
            tiles,
            tiles,
            tiles,
            tiles,
            jax.ShapeDtypeStruct(meta.shape, meta.dtype),
            jax.ShapeDtypeStruct((splits, part, part), kind),
        ],
        in_specs=[VMEM] * 7,
        out_specs=[VMEM] * 6,
        scratch_shapes=[pltpu.VMEM((splits, rows, part), kind), dma((splits,)), dma((splits,))]
        + [dma((senders,))] * 10
        + [dma((2,))],
        compiler_params=pltpu.CompilerParams(
            collective_id=0, has_side_effects=True, vmem_limit_bytes=LIMIT
        ),
        name="exchange",
    )(outgoing, meta, kept, w_query, w_key, w_value, w_out)


def attend_kernel(
    senders, splits, arrived, q_in, k_in, v_in, own_in, w_cols, image, out, pooled_out,
    q_ref, k_ref, v_ref, own, segments, att, tile_sums, message, inbox,
    sib_send, sib_recv, far_send, far_recv, fwd_send, fwd_recv, sum_send, sum_recv,
):
    owner = lax.axis_index("dp")
    mine, sibling, across = partners(splits)
    other = lax.rem(sibling + splits // 2, splits)
    rows, part = k_ref.shape
    slots, tile, _ = k_in.shape
    q_rows = Q_TILES * tile
    window = q_rows + 2 * MAX_TILES * tile
    chunk = 2 * q_rows
    chunks = rows // chunk
    pairs = part // 128
    others = [lax.rem(mine + step, splits) for step in range(1, splits)]
    greet(senders, others)

    def share(group, index, peer, send_sem, recv_sem):
        view = att.at[group, rows_of(index, chunk), :]
        return pltpu.make_async_remote_copy(
            src_ref=view,
            dst_ref=view,
            send_sem=send_sem.at[index],
            recv_sem=recv_sem.at[index],
            device_id={"mp": peer},
        )

    def spread(index):
        share(mine, index, across, far_send, far_recv).start()
        share(mine, index, sibling, sib_send, sib_recv).start()

    def relay(index):
        share(across, index, across, far_send, far_recv).wait_recv()
        share(across, index, sibling, fwd_send, fwd_recv).start()

    low = lax.broadcasted_iota(jnp.int32, (q_rows, 128), 1) < HEAD_DIM

    zero = jnp.zeros((tile, 128), jnp.bfloat16)
    low_tile = lax.broadcasted_iota(jnp.int32, (tile, 128), 1) < HEAD_DIM

    def permute(block, carry):
        for t in range(Q_TILES):
            place = arrived[block * Q_TILES + t]
            here = rows_of(block * Q_TILES + t, tile)
            query = q_in[place]
            value = v_in[place]
            k_ref[here, :] = k_in[place]
            own[here, :] = own_in[place]
            for p in range(pairs):
                pair = query[:, p * 128 : (p + 1) * 128]
                base = block * 2 * Q_TILES + t
                q_ref[p, rows_of(base, tile), :] = jnp.where(low_tile, pair, zero)
                q_ref[p, rows_of(base + Q_TILES, tile), :] = jnp.where(low_tile, zero, pair)
                v_ref[here, p * 256 : p * 256 + 128] = value[:, p * 128 : (p + 1) * 128]
                v_ref[here, p * 256 + 128 : (p + 1) * 256] = jnp.ones((tile, 128), jnp.bfloat16)
        return carry

    lax.fori_loop(0, slots // Q_TILES, permute, 0)
    spans = lax.broadcasted_iota(jnp.int32, (slots, rows), 1) // tile
    expand = (spans == lax.broadcasted_iota(jnp.int32, (slots, rows), 0)).astype(jnp.bfloat16)
    numbers = jnp.broadcast_to(image[...].astype(jnp.float32), (8, slots)).astype(jnp.bfloat16)
    segments[...] = jnp.dot(numbers, expand, preferred_element_type=jnp.float32)

    def attend(block):
        start = jnp.clip(block * q_rows - MAX_TILES * tile, 0, rows - window)
        across_rows = segments[0:1, rows_of(block, q_rows)]
        of_query = jnp.broadcast_to(across_rows, (q_rows, q_rows)).T[:, 0:1]
        of_key = segments[0:1, pl.ds(pl.multiple_of(start, q_rows), window)]
        bias = jnp.where(of_query == of_key, 0.0, -1e30)
        keys = pl.ds(pl.multiple_of(start, q_rows), window)
        for p in range(pairs):
            queries = q_ref[p, rows_of(block, 2 * q_rows), :]
            key_rows = k_ref[keys, p * 128 : (p + 1) * 128]
            values = v_ref[keys, p * 256 : (p + 1) * 256]
            scores = lax.dot_general(
                queries, key_rows, (((1,), (1,)), ((), ())), preferred_element_type=jnp.float32
            )
            halves = []
            for half in range(2):
                masked = scores[half * q_rows : (half + 1) * q_rows, :] * HEAD_DIM**-0.5 + bias
                peak = jnp.max(masked, axis=-1, keepdims=True)
                raised = jnp.exp(masked - peak).astype(jnp.bfloat16)
                mixed = jnp.dot(raised, values, preferred_element_type=jnp.float32)
                halves.append(mixed[:, :128] / mixed[:, 128:])
            att[mine, rows_of(block, q_rows), p * 128 : (p + 1) * 128] = jnp.where(
                low, halves[0], halves[1]
            ).astype(jnp.bfloat16)

    def attention_step(index, carry):
        attend(2 * index)

        @pl.when(index >= 1)
        def _():
            spread(index - 1)

        attend(2 * index + 1)

        @pl.when(index >= 4)
        def _():
            relay(index - 4)

        return carry

    lax.fori_loop(0, chunks, attention_step, 0)
    spread(chunks - 1)
    live = jnp.sum((image[...] >= 0).astype(jnp.int32), axis=1, keepdims=True) * tile
    lag = min(4, chunks)

    def output_step(index, carry):
        @pl.when(index < lag)
        def _():
            relay(chunks - lag + index)

        share(sibling, index, sibling, sib_send, sib_recv).wait_recv()
        share(other, index, sibling, fwd_send, fwd_recv).wait_recv()
        here = rows_of(index, chunk)
        total = jnp.zeros((chunk, part), jnp.float32)
        for group in range(splits):
            term = jnp.dot(att[group, here, :], w_cols[group], preferred_element_type=jnp.float32)
            total = total + term.astype(jnp.bfloat16).astype(jnp.float32)
        row = lax.broadcasted_iota(jnp.int32, (chunk, 1), 0) + index * chunk
        result = jnp.where(row < live, own[here, :].astype(jnp.float32) + total, 0.0)
        out[here, :] = result.astype(jnp.bfloat16)
        tile_sums[rows_of(index, chunk // tile), :] = jnp.sum(
            result.reshape(chunk // tile, tile, part), axis=1
        )
        return carry

    lax.fori_loop(0, chunks, output_step, 0)

    labels = lax.broadcasted_iota(jnp.int32, (IMG_OWN, slots), 0)
    member = (image[...] == labels).astype(jnp.float32)
    sums = jnp.dot(
        member, tile_sums[...], precision=lax.Precision.HIGHEST, preferred_element_type=jnp.float32
    )
    image_rows = jnp.sum(member, axis=1, keepdims=True) * float(tile)
    filled = image_rows > 0
    pooled = sums / jnp.maximum(image_rows, 1.0)
    local_sum = jnp.sum(jnp.where(filled, pooled, 0.0), axis=0, keepdims=True)
    local_count = jnp.sum(filled.astype(jnp.float32), axis=0, keepdims=True)
    message[:, :part] = jnp.broadcast_to(local_sum, (8, part))
    message[:, part:] = jnp.broadcast_to(local_count, (8, 128))

    def drain(index, carry):
        share(mine, index, across, far_send, far_recv).wait_send()
        share(mine, index, sibling, sib_send, sib_recv).wait_send()
        share(across, index, sibling, fwd_send, fwd_recv).wait_send()
        return carry

    lax.fori_loop(0, chunks, drain, 0)
    def sum_copy(target, source):
        return pltpu.make_async_remote_copy(
            src_ref=message,
            dst_ref=inbox.at[source],
            send_sem=sum_send.at[target],
            recv_sem=sum_recv.at[source],
            device_id={"dp": target},
        )

    def send_sum(step, carry):
        sum_copy(lax.rem(owner + step, senders), owner).start()
        return carry

    lax.fori_loop(1, senders, send_sum, 0)
    inbox[owner] = message[...]

    def wait_sum(step, carry):
        sum_copy(owner, lax.rem(owner + senders - step, senders)).wait_recv()
        sum_copy(lax.rem(owner + step, senders), owner).wait_send()
        return carry

    lax.fori_loop(1, senders, wait_sum, 0)
    grand = lax.fori_loop(
        0, senders, lambda i, acc: acc + inbox[i], jnp.zeros(message.shape, jnp.float32)
    )
    centre = grand[0:1, :part] / grand[0:1, part : part + 1]
    pooled_out[...] = jnp.where(filled, pooled - centre, 0.0).astype(jnp.bfloat16)


def finish_block(arrived, queries, keys, values, own, w_cols, image, senders, splits):
    slots, tile, part = keys.shape
    rows = slots * tile
    chunks = slots // (2 * Q_TILES)
    kind = keys.dtype
    dma = pltpu.SemaphoreType.DMA
    return pl.pallas_call(
        functools.partial(attend_kernel, senders, splits),
        out_shape=[
            jax.ShapeDtypeStruct((rows, part), kind),
            jax.ShapeDtypeStruct((IMG_OWN, part), kind),
        ],
        in_specs=[SMEM] + [VMEM] * 6,
        out_specs=[VMEM, VMEM],
        scratch_shapes=[
            pltpu.VMEM((part // 128, 2 * rows, 128), kind),
            pltpu.VMEM((rows, part), kind),
            pltpu.VMEM((rows, 2 * part), kind),
            pltpu.VMEM((rows, part), kind),
            pltpu.VMEM((8, rows), jnp.float32),
            pltpu.VMEM((splits, rows, part), kind),
            pltpu.VMEM((slots, part), jnp.float32),
            pltpu.VMEM((8, part + 128), jnp.float32),
            pltpu.VMEM((senders, 8, part + 128), jnp.float32),
        ]
        + [dma((chunks,))] * 6
        + [dma((senders,))] * 2,
        compiler_params=pltpu.CompilerParams(
            collective_id=1, has_side_effects=True, vmem_limit_bytes=LIMIT
        ),
        name="attend",
    )(arrived, queries, keys, values, own, w_cols, image)


def on_device(patches, dest_owner, dest_slot, packed_image, w_query, w_key, w_value, w_out):
    senders = lax.axis_size("dp")
    splits = lax.axis_size("mp")
    slots = dest_owner.shape[0]
    tile = patches.shape[0] // slots
    outgoing, meta, kept = pack(dest_owner, dest_slot, patches, senders, splits)
    queries, keys, values, own, slots_in, w_cols = exchange(
        outgoing, meta, kept, w_query, w_key, w_value, w_out, senders, splits, tile
    )
    arrived = arrival(slots_in, slots, senders)
    packed_out, pooled_out = finish_block(
        arrived, queries, keys, values, own, w_cols, packed_image[None, :], senders, splits
    )
    return (packed_out, pooled_out)


def solution(mesh):
    in_specs = (
        P("dp", None),
        P("dp"),
        P("dp"),
        P("dp"),
        P(None, "mp"),
        P(None, "mp"),
        P(None, "mp"),
        P("mp", None),
    )
    out_specs = (P("dp", "mp"), P("dp", "mp"))
    return jax.shard_map(
        on_device, mesh=mesh, in_specs=in_specs, out_specs=out_specs, check_vma=False
    )
```

```python
import functools

import jax
import jax.numpy as jnp
from jax import lax
from jax.experimental import pallas as pl
from jax.experimental.pallas import tpu as pltpu
from jax.sharding import PartitionSpec as P

HEAD_DIM = 64
IMG_OWN = 16
EPSILON = 1e-06
MAX_TILES = 16
Q_TILES = 8

VMEM = pl.BlockSpec(memory_space=pltpu.VMEM)
SMEM = pl.BlockSpec(memory_space=pltpu.SMEM)
LIMIT = 60 * 1024 * 1024


def rows_of(index, size):
    return pl.ds(pl.multiple_of(index * size, size), size)


def pack_kernel(
    senders, tile, part, owner, slot, patches, outgoing, meta, kept, part_rows, count, kept_sem, part_sem
):
    slots = owner.shape[0]
    per_owner = slots // senders
    mine = lax.axis_index("dp")
    column = pl.multiple_of(lax.axis_index("mp") * part, part)
    fetch = pltpu.make_async_copy(patches.at[:, pl.ds(column, part)], part_rows, part_sem.at[0])
    fetch.start()

    def clear(index, carry):
        count[index] = 0
        return carry

    lax.fori_loop(0, senders, clear, 0)

    def keep(source, target):
        return pltpu.make_async_copy(
            patches.at[rows_of(source, tile), :], kept.at[rows_of(target, tile), :], kept_sem.at[target]
        )

    fetch.wait()

    def place(index, carry):
        target = owner[index]
        rank = count[target]
        count[target] = rank + 1
        meta[target * 8, rank] = slot[index]
        outgoing[rows_of(target * per_owner + rank, tile), :] = part_rows[rows_of(index, tile), :]

        @pl.when(target == mine)
        def _():
            keep(index, rank).start()

        return carry

    lax.fori_loop(0, slots, place, 0, unroll=4)

    def settle(index, carry):
        keep(index, index).wait()
        return carry

    lax.fori_loop(0, per_owner, settle, 0)


def pack(owner, slot, patches, senders, splits):
    slots = owner.shape[0]
    rows, width = patches.shape
    part = width // splits
    tile = rows // slots
    dma = pltpu.SemaphoreType.DMA
    return pl.pallas_call(
        functools.partial(pack_kernel, senders, tile, part),
        out_shape=[
            jax.ShapeDtypeStruct((rows, part), patches.dtype),
            jax.ShapeDtypeStruct((senders * 8, 128), jnp.int32),
            jax.ShapeDtypeStruct((rows // senders, width), patches.dtype),
        ],
        in_specs=[SMEM, SMEM, pl.BlockSpec(memory_space=pl.ANY)],
        out_specs=[VMEM, SMEM, VMEM],
        scratch_shapes=[
            pltpu.VMEM((rows, part), patches.dtype),
            pltpu.SMEM((senders,), jnp.int32),
            dma((slots // senders,)),
            dma((1,)),
        ],
        name="pack",
    )(owner, slot, patches)


def paired(index, step, count):
    result = 0
    bit = 1
    while bit < count:
        high, flip = lax.rem(index // bit, 2), lax.rem(step // bit, 2)
        result = result + bit * (high + flip - 2 * high * flip)
        bit *= 2
    return result


def partners(splits):
    mine = lax.axis_index("mp")
    sibling = mine + 1 - 2 * lax.rem(mine, 2)
    across = lax.rem(mine + splits // 2, splits)
    return mine, sibling, across


def greet(senders, peers):
    owner = lax.axis_index("dp")
    barrier = pltpu.get_barrier_semaphore()

    def one(step, carry):
        pl.semaphore_signal(barrier, inc=1, device_id={"dp": lax.rem(owner + step, senders)})
        return carry

    lax.fori_loop(1, senders, one, 0)
    for peer in peers:
        pl.semaphore_signal(barrier, inc=1, device_id={"mp": peer})
    pl.semaphore_wait(barrier, senders - 1 + len(peers))


def exchange_kernel(
    senders, splits, tile, outgoing, meta, kept, w_query, w_key, w_value, w_out,
    q_out, k_out, v_out, own_out, arrived, w_cols, gathered, slots_in, w_send, w_recv, meta_send, meta_recv, send, recv, sib_send, sib_recv, far_send, far_recv, fwd_send, fwd_recv,
    local_sem,
):
    owner = lax.axis_index("dp")
    mine, sibling, across = partners(splits)
    rows, part = outgoing.shape
    block = rows // senders
    width = splits * part
    block_tiles = block // tile
    others = [lax.rem(mine + step, splits) for step in range(1, splits)]
    greet(senders, others)

    def meta_copy(target, source):
        return pltpu.make_async_remote_copy(
            src_ref=meta.at[rows_of(target, 8), :],
            dst_ref=slots_in.at[rows_of(source, 8), :],
            send_sem=meta_send.at[target],
            recv_sem=meta_recv.at[source],
            device_id={"dp": target},
        )

    def data_copy(target, source):
        return pltpu.make_async_remote_copy(
            src_ref=outgoing.at[rows_of(target, block), :],
            dst_ref=gathered.at[mine, rows_of(source, block), :],
            send_sem=send.at[target],
            recv_sem=recv.at[source],
            device_id={"dp": target},
        )

    def share(part, source, peer, send_sem, recv_sem):
        view = gathered.at[part, rows_of(source, block), :]
        return pltpu.make_async_remote_copy(
            src_ref=view,
            dst_ref=view,
            send_sem=send_sem.at[source],
            recv_sem=recv_sem.at[source],
            device_id={"mp": peer},
        )

    def weight_copy(target, source):
        return pltpu.make_async_remote_copy(
            src_ref=w_out.at[:, pl.ds(pl.multiple_of(target * part, part), part)],
            dst_ref=w_cols.at[source],
            send_sem=w_send.at[target],
            recv_sem=w_recv.at[source],
            device_id={"mp": target},
        )

    def start_all(step, carry):
        target = paired(owner, step, senders)
        data_copy(target, owner).start()
        meta_copy(target, owner).start()
        return carry

    lax.fori_loop(1, senders, start_all, 0)
    for target in others:
        weight_copy(target, mine).start()
    own_w = pltpu.make_async_copy(
        w_out.at[:, pl.ds(pl.multiple_of(mine * part, part), part)], w_cols.at[mine], local_sem.at[0]
    )
    own_w.start()
    own_meta = pltpu.make_async_copy(
        meta.at[rows_of(owner, 8), :], slots_in.at[rows_of(owner, 8), :], local_sem.at[1]
    )
    own_meta.start()

    def project(parts, source):
        values = jnp.concatenate(parts, axis=1).astype(jnp.float32)
        centred = values - jnp.sum(values, axis=-1, keepdims=True) * (1.0 / width)
        spread_of = jnp.sum(centred * centred, axis=-1, keepdims=True) * (1.0 / width)
        normed = (centred * lax.rsqrt(spread_of + EPSILON)).astype(jnp.bfloat16)
        here = pl.ds(source * block_tiles, block_tiles)
        for weight, result in ((w_query, q_out), (w_key, k_out), (w_value, v_out)):
            product = jnp.dot(normed, weight[...], preferred_element_type=jnp.float32)
            result[here] = product.astype(jnp.bfloat16).reshape(block_tiles, tile, part)

    def spread(source):
        share(mine, source, across, far_send, far_recv).start()
        share(mine, source, sibling, sib_send, sib_recv).start()

    def relay(source):
        share(across, source, across, far_send, far_recv).wait_recv()
        share(across, source, sibling, fwd_send, fwd_recv).start()

    other = lax.rem(sibling + splits // 2, splits)

    def source_at(step):
        return paired(owner, step, senders)

    def compute(source):
        share(sibling, source, sibling, sib_send, sib_recv).wait_recv()
        share(other, source, sibling, fwd_send, fwd_recv).wait_recv()
        here = rows_of(source, block)
        project([gathered[p, here, :] for p in range(splits)], source)
        own_out[pl.ds(source * block_tiles, block_tiles)] = gathered[mine, here, :].reshape(
            block_tiles, tile, part
        )

    project([kept[...]], owner)
    own_out[pl.ds(owner * block_tiles, block_tiles)] = outgoing[rows_of(owner, block), :].reshape(
        block_tiles, tile, part
    )

    def arrive(step, carry):
        source = source_at(step)
        data_copy(owner, source).wait_recv()
        spread(source)

        @pl.when(step >= 2)
        def _():
            relay(source_at(step - 1))

        @pl.when(step >= 3)
        def _():
            compute(source_at(step - 2))

        return carry

    lax.fori_loop(1, senders, arrive, 0)
    relay(source_at(senders - 1))

    def compute_rest(step, carry):
        compute(source_at(step))
        return carry

    lax.fori_loop(max(1, senders - 2), senders, compute_rest, 0)
    own_w.wait()
    own_meta.wait()
    for target in others:
        weight_copy(mine, target).wait_recv()
        weight_copy(target, mine).wait_send()

    def finish(step, carry):
        source = source_at(step)
        share(mine, source, across, far_send, far_recv).wait_send()
        share(mine, source, sibling, sib_send, sib_recv).wait_send()
        share(across, source, sibling, fwd_send, fwd_recv).wait_send()
        return carry

    lax.fori_loop(1, senders, finish, 0)

    def finish_peers(step, carry):
        source = source_at(step)
        target = source
        meta_copy(owner, source).wait_recv()
        meta_copy(target, owner).wait_send()
        data_copy(target, owner).wait_send()
        return carry

    lax.fori_loop(1, senders, finish_peers, 0)
    slots = rows // tile
    rank = lax.broadcasted_iota(jnp.int32, (128, slots), 0)
    target_slot = lax.broadcasted_iota(jnp.int32, (128, slots), 1)

    def locate(source, total):
        line = slots_in[rows_of(source, 8), :].astype(jnp.float32)[0:1, :]
        placed = jnp.broadcast_to(line, (128, 128)).T[:, 0:1].astype(jnp.int32)
        found = (placed == target_slot) & (rank < block_tiles)
        position = jnp.where(found, rank + source * block_tiles, 0)
        return total + jnp.sum(position, axis=0, keepdims=True)

    arrived[...] = lax.fori_loop(0, senders, locate, jnp.zeros((1, slots), jnp.int32))


def exchange(outgoing, meta, kept, w_query, w_key, w_value, w_out, senders, splits, tile):
    rows, part = outgoing.shape
    kind = outgoing.dtype
    dma = pltpu.SemaphoreType.DMA
    tiles = jax.ShapeDtypeStruct((rows // tile, tile, part), kind)
    return pl.pallas_call(
        functools.partial(exchange_kernel, senders, splits, tile),
        out_shape=[
            tiles,
            tiles,
            tiles,
            tiles,
            jax.ShapeDtypeStruct((1, rows // tile), meta.dtype),
            jax.ShapeDtypeStruct((splits, part, part), kind),
        ],
        in_specs=[VMEM] * 7,
        out_specs=[VMEM] * 6,
        scratch_shapes=[
            pltpu.VMEM((splits, rows, part), kind),
            pltpu.VMEM(meta.shape, meta.dtype),
            dma((splits,)),
            dma((splits,)),
        ]
        + [dma((senders,))] * 10
        + [dma((2,))],
        compiler_params=pltpu.CompilerParams(
            collective_id=0, has_side_effects=True, vmem_limit_bytes=LIMIT
        ),
        name="exchange",
    )(outgoing, meta, kept, w_query, w_key, w_value, w_out)


def attend_kernel(
    senders, splits, arrived, q_in, k_in, v_in, own_in, w_cols, image, out, pooled_out,
    q_ref, k_ref, v_ref, own, segments, att, tile_sums, message, inbox,
    sib_send, sib_recv, far_send, far_recv, fwd_send, fwd_recv, sum_send, sum_recv,
):
    owner = lax.axis_index("dp")
    mine, sibling, across = partners(splits)
    other = lax.rem(sibling + splits // 2, splits)
    rows, part = k_ref.shape
    slots, tile, _ = k_in.shape
    q_rows = Q_TILES * tile
    window = q_rows + 2 * MAX_TILES * tile
    chunk = q_rows
    chunks = rows // chunk
    pairs = part // 128
    others = [lax.rem(mine + step, splits) for step in range(1, splits)]
    greet(senders, others)

    def share(group, index, peer, send_sem, recv_sem):
        view = att.at[group, rows_of(index, chunk), :]
        return pltpu.make_async_remote_copy(
            src_ref=view,
            dst_ref=view,
            send_sem=send_sem.at[index],
            recv_sem=recv_sem.at[index],
            device_id={"mp": peer},
        )

    def spread(index):
        share(mine, index, across, far_send, far_recv).start()
        share(mine, index, sibling, sib_send, sib_recv).start()

    def relay(index):
        share(across, index, across, far_send, far_recv).wait_recv()
        share(across, index, sibling, fwd_send, fwd_recv).start()

    low = lax.broadcasted_iota(jnp.int32, (q_rows, 128), 1) < HEAD_DIM

    zero = jnp.zeros((tile, 128), jnp.bfloat16)
    low_tile = lax.broadcasted_iota(jnp.int32, (tile, 128), 1) < HEAD_DIM

    def permute(block, carry):
        for t in range(Q_TILES):
            place = arrived[0, block * Q_TILES + t]
            here = rows_of(block * Q_TILES + t, tile)
            query = q_in[place]
            value = v_in[place]
            k_ref[here, :] = k_in[place]
            own[here, :] = own_in[place]
            for p in range(pairs):
                pair = query[:, p * 128 : (p + 1) * 128]
                base = block * 2 * Q_TILES + t
                q_ref[p, rows_of(base, tile), :] = jnp.where(low_tile, pair, zero)
                q_ref[p, rows_of(base + Q_TILES, tile), :] = jnp.where(low_tile, zero, pair)
                v_ref[here, p * 256 : p * 256 + 128] = value[:, p * 128 : (p + 1) * 128]
                v_ref[here, p * 256 + 128 : (p + 1) * 256] = jnp.ones((tile, 128), jnp.bfloat16)
        return carry

    lax.fori_loop(0, slots // Q_TILES, permute, 0)
    spans = lax.broadcasted_iota(jnp.int32, (slots, rows), 1) // tile
    expand = (spans == lax.broadcasted_iota(jnp.int32, (slots, rows), 0)).astype(jnp.bfloat16)
    numbers = jnp.broadcast_to(image[...].astype(jnp.float32), (8, slots)).astype(jnp.bfloat16)
    segments[...] = jnp.dot(numbers, expand, preferred_element_type=jnp.float32)

    def attend(block):
        start = jnp.clip(block * q_rows - MAX_TILES * tile, 0, rows - window)
        across_rows = segments[0:1, rows_of(block, q_rows)]
        of_query = jnp.broadcast_to(across_rows, (q_rows, q_rows)).T[:, 0:1]
        of_key = segments[0:1, pl.ds(pl.multiple_of(start, q_rows), window)]
        bias = jnp.where(of_query == of_key, 0.0, -1e30)
        keys = pl.ds(pl.multiple_of(start, q_rows), window)
        for p in range(pairs):
            queries = q_ref[p, rows_of(block, 2 * q_rows), :]
            key_rows = k_ref[keys, p * 128 : (p + 1) * 128]
            values = v_ref[keys, p * 256 : (p + 1) * 256]
            scores = lax.dot_general(
                queries, key_rows, (((1,), (1,)), ((), ())), preferred_element_type=jnp.float32
            )
            halves = []
            for half in range(2):
                masked = scores[half * q_rows : (half + 1) * q_rows, :] * HEAD_DIM**-0.5 + bias
                peak = jnp.max(masked, axis=-1, keepdims=True)
                raised = jnp.exp(masked - peak).astype(jnp.bfloat16)
                mixed = jnp.dot(raised, values, preferred_element_type=jnp.float32)
                halves.append(mixed[:, :128] / mixed[:, 128:])
            att[mine, rows_of(block, q_rows), p * 128 : (p + 1) * 128] = jnp.where(
                low, halves[0], halves[1]
            ).astype(jnp.bfloat16)

    live = jnp.sum((image[...] >= 0).astype(jnp.int32), axis=1, keepdims=True) * tile
    relay_lag = min(6, chunks)
    output_lag = min(8, chunks)

    def output(index):
        share(sibling, index, sibling, sib_send, sib_recv).wait_recv()
        share(other, index, sibling, fwd_send, fwd_recv).wait_recv()
        here = rows_of(index, chunk)
        total = jnp.zeros((chunk, part), jnp.float32)
        for group in range(splits):
            term = jnp.dot(att[group, here, :], w_cols[group], preferred_element_type=jnp.float32)
            total = total + term.astype(jnp.bfloat16).astype(jnp.float32)
        row = lax.broadcasted_iota(jnp.int32, (chunk, 1), 0) + index * chunk
        result = jnp.where(row < live, own[here, :].astype(jnp.float32) + total, 0.0)
        out[here, :] = result.astype(jnp.bfloat16)
        tile_sums[rows_of(index, chunk // tile), :] = jnp.sum(
            result.reshape(chunk // tile, tile, part), axis=1
        )

    def attention_step(index, carry):
        attend(index)

        @pl.when(index >= 1)
        def _():
            spread(index - 1)

        @pl.when(index >= relay_lag)
        def _():
            relay(index - relay_lag)

        @pl.when(index >= output_lag)
        def _():
            output(index - output_lag)

        return carry

    lax.fori_loop(0, chunks, attention_step, 0)
    spread(chunks - 1)

    def output_step(index, carry):
        @pl.when(index < chunks - output_lag + relay_lag)
        def _():
            relay(index + output_lag - relay_lag)

        output(index)
        return carry

    lax.fori_loop(chunks - output_lag, chunks - output_lag + relay_lag, output_step, 0)

    def rest(index, carry):
        output(index)
        return carry

    lax.fori_loop(chunks - output_lag + relay_lag, chunks, rest, 0)
    labels = lax.broadcasted_iota(jnp.int32, (IMG_OWN, slots), 0)
    member = (image[...] == labels).astype(jnp.float32)
    sums = jnp.dot(
        member, tile_sums[...], precision=lax.Precision.HIGHEST, preferred_element_type=jnp.float32
    )
    image_rows = jnp.sum(member, axis=1, keepdims=True) * float(tile)
    filled = image_rows > 0
    pooled = sums / jnp.maximum(image_rows, 1.0)
    local_sum = jnp.sum(jnp.where(filled, pooled, 0.0), axis=0, keepdims=True)
    local_count = jnp.sum(filled.astype(jnp.float32), axis=0, keepdims=True)
    message[:, :part] = jnp.broadcast_to(local_sum, (8, part))
    message[:, part:] = jnp.broadcast_to(local_count, (8, 128))

    def drain(index, carry):
        share(mine, index, across, far_send, far_recv).wait_send()
        share(mine, index, sibling, sib_send, sib_recv).wait_send()
        share(across, index, sibling, fwd_send, fwd_recv).wait_send()
        return carry

    lax.fori_loop(0, chunks, drain, 0)
    def sum_copy(target, source):
        return pltpu.make_async_remote_copy(
            src_ref=message,
            dst_ref=inbox.at[source],
            send_sem=sum_send.at[target],
            recv_sem=sum_recv.at[source],
            device_id={"dp": target},
        )

    def send_sum(step, carry):
        sum_copy(lax.rem(owner + step, senders), owner).start()
        return carry

    lax.fori_loop(1, senders, send_sum, 0)
    inbox[owner] = message[...]

    def wait_sum(step, carry):
        sum_copy(owner, lax.rem(owner + senders - step, senders)).wait_recv()
        sum_copy(lax.rem(owner + step, senders), owner).wait_send()
        return carry

    lax.fori_loop(1, senders, wait_sum, 0)
    grand = lax.fori_loop(
        0, senders, lambda i, acc: acc + inbox[i], jnp.zeros(message.shape, jnp.float32)
    )
    centre = grand[0:1, :part] / grand[0:1, part : part + 1]
    pooled_out[...] = jnp.where(filled, pooled - centre, 0.0).astype(jnp.bfloat16)


def finish_block(arrived, queries, keys, values, own, w_cols, image, senders, splits):
    slots, tile, part = keys.shape
    rows = slots * tile
    chunks = slots // Q_TILES
    kind = keys.dtype
    dma = pltpu.SemaphoreType.DMA
    return pl.pallas_call(
        functools.partial(attend_kernel, senders, splits),
        out_shape=[
            jax.ShapeDtypeStruct((rows, part), kind),
            jax.ShapeDtypeStruct((IMG_OWN, part), kind),
        ],
        in_specs=[SMEM] + [VMEM] * 6,
        out_specs=[VMEM, VMEM],
        scratch_shapes=[
            pltpu.VMEM((part // 128, 2 * rows, 128), kind),
            pltpu.VMEM((rows, part), kind),
            pltpu.VMEM((rows, 2 * part), kind),
            pltpu.VMEM((rows, part), kind),
            pltpu.VMEM((8, rows), jnp.float32),
            pltpu.VMEM((splits, rows, part), kind),
            pltpu.VMEM((slots, part), jnp.float32),
            pltpu.VMEM((8, part + 128), jnp.float32),
            pltpu.VMEM((senders, 8, part + 128), jnp.float32),
        ]
        + [dma((chunks,))] * 6
        + [dma((senders,))] * 2,
        compiler_params=pltpu.CompilerParams(
            collective_id=1, has_side_effects=True, vmem_limit_bytes=LIMIT
        ),
        name="attend",
    )(arrived, queries, keys, values, own, w_cols, image)


def hand_kernel(rows, pooled, rows_out, pooled_out):
    rows_out[...] = rows[...]
    pooled_out[...] = pooled[...]


def hand_over(rows, pooled):
    steps = 4
    big = pl.BlockSpec((rows.shape[0] // steps, rows.shape[1]), lambda i: (i, 0))
    small = pl.BlockSpec(pooled.shape, lambda i: (0, 0))
    return pl.pallas_call(
        hand_kernel,
        grid=(steps,),
        out_shape=[
            jax.ShapeDtypeStruct(rows.shape, rows.dtype),
            jax.ShapeDtypeStruct(pooled.shape, pooled.dtype),
        ],
        in_specs=[big, small],
        out_specs=[big, small],
        name="hand_over",
    )(rows, pooled)


def on_device(patches, dest_owner, dest_slot, packed_image, w_query, w_key, w_value, w_out):
    senders = lax.axis_size("dp")
    splits = lax.axis_size("mp")
    slots = dest_owner.shape[0]
    tile = patches.shape[0] // slots
    outgoing, meta, kept = pack(dest_owner, dest_slot, patches, senders, splits)
    queries, keys, values, own, arrived, w_cols = exchange(
        outgoing, meta, kept, w_query, w_key, w_value, w_out, senders, splits, tile
    )
    packed_out, pooled_out = finish_block(
        arrived, queries, keys, values, own, w_cols, packed_image[None, :], senders, splits
    )
    return hand_over(packed_out, pooled_out)


def solution(mesh):
    in_specs = (
        P("dp", None),
        P("dp"),
        P("dp"),
        P("dp"),
        P(None, "mp"),
        P(None, "mp"),
        P(None, "mp"),
        P("mp", None),
    )
    out_specs = (P("dp", "mp"), P("dp", "mp"))
    return jax.shard_map(
        on_device, mesh=mesh, in_specs=in_specs, out_specs=out_specs, check_vma=False
    )
```

```python
import functools

import jax
import jax.numpy as jnp
from jax import lax
from jax.experimental import pallas as pl
from jax.experimental.pallas import tpu as pltpu
from jax.sharding import PartitionSpec as P

HEAD_DIM = 64
IMG_OWN = 16
EPSILON = 1e-06
MAX_TILES = 16
Q_TILES = 8

VMEM = pl.BlockSpec(memory_space=pltpu.VMEM)
SMEM = pl.BlockSpec(memory_space=pltpu.SMEM)
LIMIT = 60 * 1024 * 1024


def rows_of(index, size):
    return pl.ds(pl.multiple_of(index * size, size), size)


def pack_kernel(
    senders, tile, part, owner, slot, patches, outgoing, meta, kept, part_rows, count, kept_sem, part_sem
):
    slots = owner.shape[0]
    per_owner = slots // senders
    mine = lax.axis_index("dp")
    column = pl.multiple_of(lax.axis_index("mp") * part, part)
    fetch = pltpu.make_async_copy(patches.at[:, pl.ds(column, part)], part_rows, part_sem.at[0])
    fetch.start()

    def clear(index, carry):
        count[index] = 0
        return carry

    lax.fori_loop(0, senders, clear, 0)

    def keep(source, target):
        return pltpu.make_async_copy(
            patches.at[rows_of(source, tile), :], kept.at[rows_of(target, tile), :], kept_sem.at[target]
        )

    fetch.wait()

    def place(index, carry):
        target = owner[index]
        rank = count[target]
        count[target] = rank + 1
        meta[target * 8, rank] = slot[index]
        outgoing[rows_of(target * per_owner + rank, tile), :] = part_rows[rows_of(index, tile), :]

        @pl.when(target == mine)
        def _():
            keep(index, rank).start()

        return carry

    lax.fori_loop(0, slots, place, 0, unroll=4)

    def settle(index, carry):
        keep(index, index).wait()
        return carry

    lax.fori_loop(0, per_owner, settle, 0)


def pack(owner, slot, patches, senders, splits):
    slots = owner.shape[0]
    rows, width = patches.shape
    part = width // splits
    tile = rows // slots
    dma = pltpu.SemaphoreType.DMA
    return pl.pallas_call(
        functools.partial(pack_kernel, senders, tile, part),
        out_shape=[
            jax.ShapeDtypeStruct((rows, part), patches.dtype),
            jax.ShapeDtypeStruct((senders * 8, 128), jnp.int32),
            jax.ShapeDtypeStruct((rows // senders, width), patches.dtype),
        ],
        in_specs=[SMEM, SMEM, pl.BlockSpec(memory_space=pl.ANY)],
        out_specs=[VMEM, SMEM, VMEM],
        scratch_shapes=[
            pltpu.VMEM((rows, part), patches.dtype),
            pltpu.SMEM((senders,), jnp.int32),
            dma((slots // senders,)),
            dma((1,)),
        ],
        name="pack",
    )(owner, slot, patches)


def paired(index, step, count):
    result = 0
    bit = 1
    while bit < count:
        high, flip = lax.rem(index // bit, 2), lax.rem(step // bit, 2)
        result = result + bit * (high + flip - 2 * high * flip)
        bit *= 2
    return result


def partners(splits):
    mine = lax.axis_index("mp")
    sibling = mine + 1 - 2 * lax.rem(mine, 2)
    across = lax.rem(mine + splits // 2, splits)
    return mine, sibling, across


def greet(senders, peers):
    owner = lax.axis_index("dp")
    barrier = pltpu.get_barrier_semaphore()

    def one(step, carry):
        pl.semaphore_signal(barrier, inc=1, device_id={"dp": lax.rem(owner + step, senders)})
        return carry

    lax.fori_loop(1, senders, one, 0)
    for peer in peers:
        pl.semaphore_signal(barrier, inc=1, device_id={"mp": peer})
    pl.semaphore_wait(barrier, senders - 1 + len(peers))


def exchange_kernel(
    senders, splits, tile, outgoing, meta, kept, w_query, w_key, w_value, w_out,
    q_out, k_out, v_out, own_out, arrived, w_cols, gathered, slots_in, q_mat, k_mat, v_mat, w_mat, mat_sem, w_send, w_recv, meta_send, meta_recv, send, recv, sib_send, sib_recv, far_send, far_recv, fwd_send, fwd_recv,
    local_sem,
):
    owner = lax.axis_index("dp")
    mine, sibling, across = partners(splits)
    rows, part = outgoing.shape
    block = rows // senders
    width = splits * part
    block_tiles = block // tile
    halves = 2
    units = halves * senders
    piece = block // halves
    others = [lax.rem(mine + step, splits) for step in range(1, splits)]
    loads = [
        pltpu.make_async_copy(source, target, mat_sem.at[i])
        for i, (source, target) in enumerate(
            ((w_out, w_mat), (w_query, q_mat), (w_key, k_mat), (w_value, v_mat))
        )
    ]
    for load in loads:
        load.start()
    greet(senders, others)

    def meta_copy(target, source):
        return pltpu.make_async_remote_copy(
            src_ref=meta.at[rows_of(target, 8), :],
            dst_ref=slots_in.at[rows_of(source, 8), :],
            send_sem=meta_send.at[target],
            recv_sem=meta_recv.at[source],
            device_id={"dp": target},
        )

    def data_copy(target, source):
        return pltpu.make_async_remote_copy(
            src_ref=outgoing.at[rows_of(target, piece), :],
            dst_ref=gathered.at[mine, rows_of(source, piece), :],
            send_sem=send.at[target],
            recv_sem=recv.at[source],
            device_id={"dp": target // halves},
        )

    def share(part, source, peer, send_sem, recv_sem):
        view = gathered.at[part, rows_of(source, piece), :]
        return pltpu.make_async_remote_copy(
            src_ref=view,
            dst_ref=view,
            send_sem=send_sem.at[source],
            recv_sem=recv_sem.at[source],
            device_id={"mp": peer},
        )

    def weight_copy(target, source):
        return pltpu.make_async_remote_copy(
            src_ref=w_mat.at[:, pl.ds(pl.multiple_of(target * part, part), part)],
            dst_ref=w_cols.at[source],
            send_sem=w_send.at[target],
            recv_sem=w_recv.at[source],
            device_id={"mp": target},
        )

    def start_all(step, carry):
        target = paired(owner, step, senders)
        for half in range(halves):
            data_copy(target * halves + half, owner * halves + half).start()
        meta_copy(target, owner).start()
        return carry

    lax.fori_loop(1, senders, start_all, 0)
    loads[0].wait()
    for target in others:
        weight_copy(target, mine).start()
    own_w = pltpu.make_async_copy(
        w_mat.at[:, pl.ds(pl.multiple_of(mine * part, part), part)], w_cols.at[mine], local_sem.at[0]
    )
    own_w.start()
    own_meta = pltpu.make_async_copy(
        meta.at[rows_of(owner, 8), :], slots_in.at[rows_of(owner, 8), :], local_sem.at[1]
    )
    own_meta.start()

    def project(parts, source):
        values = jnp.concatenate(parts, axis=1).astype(jnp.float32)
        centred = values - jnp.sum(values, axis=-1, keepdims=True) * (1.0 / width)
        spread_of = jnp.sum(centred * centred, axis=-1, keepdims=True) * (1.0 / width)
        normed = (centred * lax.rsqrt(spread_of + EPSILON)).astype(jnp.bfloat16)
        count = parts[0].shape[0] // tile
        here = pl.ds(source * count, count)
        for weight, result in ((q_mat, q_out), (k_mat, k_out), (v_mat, v_out)):
            product = jnp.dot(normed, weight[...], preferred_element_type=jnp.float32)
            result[here] = product.astype(jnp.bfloat16).reshape(count, tile, part)

    def spread(source):
        share(mine, source, across, far_send, far_recv).start()
        share(mine, source, sibling, sib_send, sib_recv).start()

    def relay(source):
        share(across, source, across, far_send, far_recv).wait_recv()
        share(across, source, sibling, fwd_send, fwd_recv).start()

    other = lax.rem(sibling + splits // 2, splits)

    def source_at(step):
        return paired(owner, step, senders)

    def unit_at(step):
        return source_at(step // halves) * halves + lax.rem(step, halves)

    def compute(source):
        share(sibling, source, sibling, sib_send, sib_recv).wait_recv()
        share(other, source, sibling, fwd_send, fwd_recv).wait_recv()
        here = rows_of(source, piece)
        project([gathered[p, here, :] for p in range(splits)], source)
        count = piece // tile
        own_out[pl.ds(source * count, count)] = gathered[mine, here, :].reshape(count, tile, part)

    for load in loads[1:]:
        load.wait()
    project([kept[...]], owner)
    own_out[pl.ds(owner * block_tiles, block_tiles)] = outgoing[rows_of(owner, block), :].reshape(
        block_tiles, tile, part
    )

    def arrive(step, carry):
        unit = unit_at(step)
        data_copy(owner * halves + lax.rem(step, halves), unit).wait_recv()
        spread(unit)

        @pl.when(step >= halves + 1)
        def _():
            relay(unit_at(step - 1))

        @pl.when(step >= halves + 2)
        def _():
            compute(unit_at(step - 2))

        return carry

    lax.fori_loop(halves, units, arrive, 0)
    relay(unit_at(units - 1))

    def compute_rest(step, carry):
        compute(unit_at(step))
        return carry

    lax.fori_loop(units - 2, units, compute_rest, 0)
    own_w.wait()
    own_meta.wait()
    for target in others:
        weight_copy(mine, target).wait_recv()
        weight_copy(target, mine).wait_send()

    def finish(step, carry):
        source = unit_at(step)
        share(mine, source, across, far_send, far_recv).wait_send()
        share(mine, source, sibling, sib_send, sib_recv).wait_send()
        share(across, source, sibling, fwd_send, fwd_recv).wait_send()
        return carry

    lax.fori_loop(halves, units, finish, 0)

    def finish_peers(step, carry):
        source = source_at(step)
        target = source
        meta_copy(owner, source).wait_recv()
        meta_copy(target, owner).wait_send()
        for half in range(halves):
            data_copy(target * halves + half, owner * halves + half).wait_send()
        return carry

    lax.fori_loop(1, senders, finish_peers, 0)
    slots = rows // tile
    rank = lax.broadcasted_iota(jnp.int32, (128, slots), 0)
    target_slot = lax.broadcasted_iota(jnp.int32, (128, slots), 1)

    def locate(source, total):
        line = slots_in[rows_of(source, 8), :].astype(jnp.float32)[0:1, :]
        placed = jnp.broadcast_to(line, (128, 128)).T[:, 0:1].astype(jnp.int32)
        found = (placed == target_slot) & (rank < block_tiles)
        position = jnp.where(found, rank + source * block_tiles, 0)
        return total + jnp.sum(position, axis=0, keepdims=True)

    arrived[...] = lax.fori_loop(0, senders, locate, jnp.zeros((1, slots), jnp.int32))


def exchange(outgoing, meta, kept, w_query, w_key, w_value, w_out, senders, splits, tile):
    rows, part = outgoing.shape
    kind = outgoing.dtype
    dma = pltpu.SemaphoreType.DMA
    tiles = jax.ShapeDtypeStruct((rows // tile, tile, part), kind)
    return pl.pallas_call(
        functools.partial(exchange_kernel, senders, splits, tile),
        out_shape=[
            tiles,
            tiles,
            tiles,
            tiles,
            jax.ShapeDtypeStruct((1, rows // tile), meta.dtype),
            jax.ShapeDtypeStruct((splits, part, part), kind),
        ],
        in_specs=[VMEM] * 3 + [pl.BlockSpec(memory_space=pl.ANY)] * 4,
        out_specs=[VMEM] * 6,
        scratch_shapes=[
            pltpu.VMEM((splits, rows, part), kind),
            pltpu.VMEM(meta.shape, meta.dtype),
            pltpu.VMEM(w_query.shape, kind),
            pltpu.VMEM(w_key.shape, kind),
            pltpu.VMEM(w_value.shape, kind),
            pltpu.VMEM(w_out.shape, kind),
            dma((4,)),
            dma((splits,)),
            dma((splits,)),
        ]
        + [dma((senders,))] * 2
        + [dma((2 * senders,))] * 8
        + [dma((2,))],
        compiler_params=pltpu.CompilerParams(
            collective_id=0, has_side_effects=True, vmem_limit_bytes=LIMIT
        ),
        name="exchange",
    )(outgoing, meta, kept, w_query, w_key, w_value, w_out)


def attend_kernel(
    senders, splits, arrived, q_in, k_in, v_in, own_in, w_cols, image, out, pooled_out,
    q_ref, k_ref, v_ref, own, segments, att, tile_sums, message, inbox,
    sib_send, sib_recv, far_send, far_recv, fwd_send, fwd_recv, sum_send, sum_recv,
):
    owner = lax.axis_index("dp")
    mine, sibling, across = partners(splits)
    other = lax.rem(sibling + splits // 2, splits)
    rows, part = k_ref.shape
    slots, tile, _ = k_in.shape
    q_rows = Q_TILES * tile
    window = q_rows + 2 * MAX_TILES * tile
    chunk = q_rows
    chunks = rows // chunk
    pairs = part // 128
    others = [lax.rem(mine + step, splits) for step in range(1, splits)]
    greet(senders, others)

    def share(group, index, peer, send_sem, recv_sem):
        view = att.at[group, rows_of(index, chunk), :]
        return pltpu.make_async_remote_copy(
            src_ref=view,
            dst_ref=view,
            send_sem=send_sem.at[index],
            recv_sem=recv_sem.at[index],
            device_id={"mp": peer},
        )

    def spread(index):
        share(mine, index, across, far_send, far_recv).start()
        share(mine, index, sibling, sib_send, sib_recv).start()

    def relay(index):
        share(across, index, across, far_send, far_recv).wait_recv()
        share(across, index, sibling, fwd_send, fwd_recv).start()

    low = lax.broadcasted_iota(jnp.int32, (q_rows, 128), 1) < HEAD_DIM

    zero = jnp.zeros((tile, 128), jnp.bfloat16)
    low_tile = lax.broadcasted_iota(jnp.int32, (tile, 128), 1) < HEAD_DIM

    def permute(block, carry):
        for t in range(Q_TILES):
            place = arrived[0, block * Q_TILES + t]
            here = rows_of(block * Q_TILES + t, tile)
            query = q_in[place]
            value = v_in[place]
            k_ref[here, :] = k_in[place]
            own[here, :] = own_in[place]
            for p in range(pairs):
                pair = query[:, p * 128 : (p + 1) * 128]
                base = block * 2 * Q_TILES + t
                q_ref[p, rows_of(base, tile), :] = jnp.where(low_tile, pair, zero)
                q_ref[p, rows_of(base + Q_TILES, tile), :] = jnp.where(low_tile, zero, pair)
                v_ref[here, p * 256 : p * 256 + 128] = value[:, p * 128 : (p + 1) * 128]
                v_ref[here, p * 256 + 128 : (p + 1) * 256] = jnp.ones((tile, 128), jnp.bfloat16)
        return carry

    lax.fori_loop(0, slots // Q_TILES, permute, 0)
    spans = lax.broadcasted_iota(jnp.int32, (slots, rows), 1) // tile
    expand = (spans == lax.broadcasted_iota(jnp.int32, (slots, rows), 0)).astype(jnp.bfloat16)
    numbers = jnp.broadcast_to(image[...].astype(jnp.float32), (8, slots)).astype(jnp.bfloat16)
    segments[...] = jnp.dot(numbers, expand, preferred_element_type=jnp.float32)

    def attend(block):
        start = jnp.clip(block * q_rows - MAX_TILES * tile, 0, rows - window)
        across_rows = segments[0:1, rows_of(block, q_rows)]
        of_query = jnp.broadcast_to(across_rows, (q_rows, q_rows)).T[:, 0:1]
        of_key = segments[0:1, pl.ds(pl.multiple_of(start, q_rows), window)]
        bias = jnp.where(of_query == of_key, 0.0, -1e30)
        keys = pl.ds(pl.multiple_of(start, q_rows), window)
        for p in range(pairs):
            queries = q_ref[p, rows_of(block, 2 * q_rows), :]
            key_rows = k_ref[keys, p * 128 : (p + 1) * 128]
            values = v_ref[keys, p * 256 : (p + 1) * 256]
            scores = lax.dot_general(
                queries, key_rows, (((1,), (1,)), ((), ())), preferred_element_type=jnp.float32
            )
            halves = []
            for half in range(2):
                masked = scores[half * q_rows : (half + 1) * q_rows, :] * HEAD_DIM**-0.5 + bias
                peak = jnp.max(masked, axis=-1, keepdims=True)
                raised = jnp.exp(masked - peak).astype(jnp.bfloat16)
                mixed = jnp.dot(raised, values, preferred_element_type=jnp.float32)
                halves.append(mixed[:, :128] / mixed[:, 128:])
            att[mine, rows_of(block, q_rows), p * 128 : (p + 1) * 128] = jnp.where(
                low, halves[0], halves[1]
            ).astype(jnp.bfloat16)

    live = jnp.sum((image[...] >= 0).astype(jnp.int32), axis=1, keepdims=True) * tile
    relay_lag = min(6, chunks)
    output_lag = min(8, chunks)

    def output(index):
        share(sibling, index, sibling, sib_send, sib_recv).wait_recv()
        share(other, index, sibling, fwd_send, fwd_recv).wait_recv()
        here = rows_of(index, chunk)
        total = jnp.zeros((chunk, part), jnp.float32)
        for group in range(splits):
            term = jnp.dot(att[group, here, :], w_cols[group], preferred_element_type=jnp.float32)
            total = total + term.astype(jnp.bfloat16).astype(jnp.float32)
        row = lax.broadcasted_iota(jnp.int32, (chunk, 1), 0) + index * chunk
        result = jnp.where(row < live, own[here, :].astype(jnp.float32) + total, 0.0)
        out[here, :] = result.astype(jnp.bfloat16)
        tile_sums[rows_of(index, chunk // tile), :] = jnp.sum(
            result.reshape(chunk // tile, tile, part), axis=1
        )

    def attention_step(index, carry):
        attend(index)

        @pl.when(index >= 1)
        def _():
            spread(index - 1)

        @pl.when(index >= relay_lag)
        def _():
            relay(index - relay_lag)

        @pl.when(index >= output_lag)
        def _():
            output(index - output_lag)

        return carry

    lax.fori_loop(0, chunks, attention_step, 0)
    spread(chunks - 1)

    def output_step(index, carry):
        @pl.when(index < chunks - output_lag + relay_lag)
        def _():
            relay(index + output_lag - relay_lag)

        output(index)
        return carry

    lax.fori_loop(chunks - output_lag, chunks - output_lag + relay_lag, output_step, 0)

    def rest(index, carry):
        output(index)
        return carry

    lax.fori_loop(chunks - output_lag + relay_lag, chunks, rest, 0)
    labels = lax.broadcasted_iota(jnp.int32, (IMG_OWN, slots), 0)
    member = (image[...] == labels).astype(jnp.float32)
    sums = jnp.dot(
        member, tile_sums[...], precision=lax.Precision.HIGHEST, preferred_element_type=jnp.float32
    )
    image_rows = jnp.sum(member, axis=1, keepdims=True) * float(tile)
    filled = image_rows > 0
    pooled = sums / jnp.maximum(image_rows, 1.0)
    local_sum = jnp.sum(jnp.where(filled, pooled, 0.0), axis=0, keepdims=True)
    local_count = jnp.sum(filled.astype(jnp.float32), axis=0, keepdims=True)
    message[:, :part] = jnp.broadcast_to(local_sum, (8, part))
    message[:, part:] = jnp.broadcast_to(local_count, (8, 128))

    def drain(index, carry):
        share(mine, index, across, far_send, far_recv).wait_send()
        share(mine, index, sibling, sib_send, sib_recv).wait_send()
        share(across, index, sibling, fwd_send, fwd_recv).wait_send()
        return carry

    lax.fori_loop(0, chunks, drain, 0)
    def sum_copy(target, source):
        return pltpu.make_async_remote_copy(
            src_ref=message,
            dst_ref=inbox.at[source],
            send_sem=sum_send.at[target],
            recv_sem=sum_recv.at[source],
            device_id={"dp": target},
        )

    def send_sum(step, carry):
        sum_copy(lax.rem(owner + step, senders), owner).start()
        return carry

    lax.fori_loop(1, senders, send_sum, 0)
    inbox[owner] = message[...]

    def wait_sum(step, carry):
        sum_copy(owner, lax.rem(owner + senders - step, senders)).wait_recv()
        sum_copy(lax.rem(owner + step, senders), owner).wait_send()
        return carry

    lax.fori_loop(1, senders, wait_sum, 0)
    grand = lax.fori_loop(
        0, senders, lambda i, acc: acc + inbox[i], jnp.zeros(message.shape, jnp.float32)
    )
    centre = grand[0:1, :part] / grand[0:1, part : part + 1]
    pooled_out[...] = jnp.where(filled, pooled - centre, 0.0).astype(jnp.bfloat16)


def finish_block(arrived, queries, keys, values, own, w_cols, image, senders, splits):
    slots, tile, part = keys.shape
    rows = slots * tile
    chunks = slots // Q_TILES
    kind = keys.dtype
    dma = pltpu.SemaphoreType.DMA
    return pl.pallas_call(
        functools.partial(attend_kernel, senders, splits),
        out_shape=[
            jax.ShapeDtypeStruct((rows, part), kind),
            jax.ShapeDtypeStruct((IMG_OWN, part), kind),
        ],
        in_specs=[SMEM] + [VMEM] * 6,
        out_specs=[VMEM, VMEM],
        scratch_shapes=[
            pltpu.VMEM((part // 128, 2 * rows, 128), kind),
            pltpu.VMEM((rows, part), kind),
            pltpu.VMEM((rows, 2 * part), kind),
            pltpu.VMEM((rows, part), kind),
            pltpu.VMEM((8, rows), jnp.float32),
            pltpu.VMEM((splits, rows, part), kind),
            pltpu.VMEM((slots, part), jnp.float32),
            pltpu.VMEM((8, part + 128), jnp.float32),
            pltpu.VMEM((senders, 8, part + 128), jnp.float32),
        ]
        + [dma((chunks,))] * 6
        + [dma((senders,))] * 2,
        compiler_params=pltpu.CompilerParams(
            collective_id=1, has_side_effects=True, vmem_limit_bytes=LIMIT
        ),
        name="attend",
    )(arrived, queries, keys, values, own, w_cols, image)


def hand_kernel(rows, pooled, rows_out, pooled_out):
    rows_out[...] = rows[...]
    pooled_out[...] = pooled[...]


def hand_over(rows, pooled):
    steps = 2
    big = pl.BlockSpec((rows.shape[0] // steps, rows.shape[1]), lambda i: (i, 0))
    small = pl.BlockSpec(pooled.shape, lambda i: (0, 0))
    return pl.pallas_call(
        hand_kernel,
        grid=(steps,),
        out_shape=[
            jax.ShapeDtypeStruct(rows.shape, rows.dtype),
            jax.ShapeDtypeStruct(pooled.shape, pooled.dtype),
        ],
        in_specs=[big, small],
        out_specs=[big, small],
        name="hand_over",
    )(rows, pooled)


def on_device(patches, dest_owner, dest_slot, packed_image, w_query, w_key, w_value, w_out):
    senders = lax.axis_size("dp")
    splits = lax.axis_size("mp")
    slots = dest_owner.shape[0]
    tile = patches.shape[0] // slots
    outgoing, meta, kept = pack(dest_owner, dest_slot, patches, senders, splits)
    queries, keys, values, own, arrived, w_cols = exchange(
        outgoing, meta, kept, w_query, w_key, w_value, w_out, senders, splits, tile
    )
    packed_out, pooled_out = finish_block(
        arrived, queries, keys, values, own, w_cols, packed_image[None, :], senders, splits
    )
    return hand_over(packed_out, pooled_out)


def solution(mesh):
    in_specs = (
        P("dp", None),
        P("dp"),
        P("dp"),
        P("dp"),
        P(None, "mp"),
        P(None, "mp"),
        P(None, "mp"),
        P("mp", None),
    )
    out_specs = (P("dp", "mp"), P("dp", "mp"))
    return jax.shard_map(
        on_device, mesh=mesh, in_specs=in_specs, out_specs=out_specs, check_vma=False
    )
```

```python
import functools

import jax
import jax.numpy as jnp
from jax import lax
from jax.experimental import pallas as pl
from jax.experimental.pallas import tpu as pltpu
from jax.sharding import PartitionSpec as P

HEAD_DIM = 64
IMG_OWN = 16
EPSILON = 1e-06
MAX_TILES = 16
Q_TILES = 8

VMEM = pl.BlockSpec(memory_space=pltpu.VMEM)
SMEM = pl.BlockSpec(memory_space=pltpu.SMEM)
LIMIT = 60 * 1024 * 1024


def rows_of(index, size):
    return pl.ds(pl.multiple_of(index * size, size), size)


def pack_kernel(
    senders, tile, part, owner, slot, patches, outgoing, meta, kept, part_rows, count, kept_sem, part_sem
):
    slots = owner.shape[0]
    per_owner = slots // senders
    mine = lax.axis_index("dp")
    column = pl.multiple_of(lax.axis_index("mp") * part, part)
    fetch = pltpu.make_async_copy(patches.at[:, pl.ds(column, part)], part_rows, part_sem.at[0])
    fetch.start()

    def clear(index, carry):
        count[index] = 0
        return carry

    lax.fori_loop(0, senders, clear, 0)

    def keep(source, target):
        return pltpu.make_async_copy(
            patches.at[rows_of(source, tile), :], kept.at[rows_of(target, tile), :], kept_sem.at[target]
        )

    fetch.wait()

    def place(index, carry):
        target = owner[index]
        rank = count[target]
        count[target] = rank + 1
        meta[target * 8, rank] = slot[index]
        outgoing[rows_of(target * per_owner + rank, tile), :] = part_rows[rows_of(index, tile), :]

        @pl.when(target == mine)
        def _():
            keep(index, rank).start()

        return carry

    lax.fori_loop(0, slots, place, 0, unroll=4)

    def settle(index, carry):
        keep(index, index).wait()
        return carry

    lax.fori_loop(0, per_owner, settle, 0)


def pack(owner, slot, patches, senders, splits):
    slots = owner.shape[0]
    rows, width = patches.shape
    part = width // splits
    tile = rows // slots
    dma = pltpu.SemaphoreType.DMA
    return pl.pallas_call(
        functools.partial(pack_kernel, senders, tile, part),
        out_shape=[
            jax.ShapeDtypeStruct((rows, part), patches.dtype),
            jax.ShapeDtypeStruct((senders * 8, 128), jnp.int32),
            jax.ShapeDtypeStruct((rows // senders, width), patches.dtype),
        ],
        in_specs=[SMEM, SMEM, pl.BlockSpec(memory_space=pl.ANY)],
        out_specs=[VMEM, SMEM, VMEM],
        scratch_shapes=[
            pltpu.VMEM((rows, part), patches.dtype),
            pltpu.SMEM((senders,), jnp.int32),
            dma((slots // senders,)),
            dma((1,)),
        ],
        name="pack",
    )(owner, slot, patches)


def paired(index, step, count):
    result = 0
    bit = 1
    while bit < count:
        high, flip = lax.rem(index // bit, 2), lax.rem(step // bit, 2)
        result = result + bit * (high + flip - 2 * high * flip)
        bit *= 2
    return result


def partners(splits):
    mine = lax.axis_index("mp")
    sibling = mine + 1 - 2 * lax.rem(mine, 2)
    across = lax.rem(mine + splits // 2, splits)
    return mine, sibling, across


def greet(senders, peers):
    owner = lax.axis_index("dp")
    barrier = pltpu.get_barrier_semaphore()

    def one(step, carry):
        pl.semaphore_signal(barrier, inc=1, device_id={"dp": lax.rem(owner + step, senders)})
        return carry

    lax.fori_loop(1, senders, one, 0)
    for peer in peers:
        pl.semaphore_signal(barrier, inc=1, device_id={"mp": peer})
    pl.semaphore_wait(barrier, senders - 1 + len(peers))


def exchange_kernel(
    senders, splits, tile, outgoing, meta, kept, w_query, w_key, w_value, w_out,
    q_out, k_out, v_out, own_out, arrived, w_cols, gathered, slots_in, q_mat, k_mat, v_mat, w_mat, mat_sem, w_send, w_recv, meta_send, meta_recv, send, recv, sib_send, sib_recv, far_send, far_recv, fwd_send, fwd_recv,
    local_sem,
):
    owner = lax.axis_index("dp")
    mine, sibling, across = partners(splits)
    rows, part = outgoing.shape
    block = rows // senders
    width = splits * part
    block_tiles = block // tile
    others = [lax.rem(mine + step, splits) for step in range(1, splits)]
    loads = [
        pltpu.make_async_copy(source, target, mat_sem.at[i])
        for i, (source, target) in enumerate(
            ((w_out, w_mat), (w_query, q_mat), (w_key, k_mat), (w_value, v_mat))
        )
    ]
    for load in loads:
        load.start()
    greet(senders, others)

    def meta_copy(target, source):
        return pltpu.make_async_remote_copy(
            src_ref=meta.at[rows_of(target, 8), :],
            dst_ref=slots_in.at[rows_of(source, 8), :],
            send_sem=meta_send.at[target],
            recv_sem=meta_recv.at[source],
            device_id={"dp": target},
        )

    def data_copy(target, source):
        return pltpu.make_async_remote_copy(
            src_ref=outgoing.at[rows_of(target, block), :],
            dst_ref=gathered.at[mine, rows_of(source, block), :],
            send_sem=send.at[target],
            recv_sem=recv.at[source],
            device_id={"dp": target},
        )

    def share(part, source, peer, send_sem, recv_sem):
        view = gathered.at[part, rows_of(source, block), :]
        return pltpu.make_async_remote_copy(
            src_ref=view,
            dst_ref=view,
            send_sem=send_sem.at[source],
            recv_sem=recv_sem.at[source],
            device_id={"mp": peer},
        )

    def weight_copy(target, source):
        return pltpu.make_async_remote_copy(
            src_ref=w_mat.at[:, pl.ds(pl.multiple_of(target * part, part), part)],
            dst_ref=w_cols.at[source],
            send_sem=w_send.at[target],
            recv_sem=w_recv.at[source],
            device_id={"mp": target},
        )

    def start_all(step, carry):
        target = paired(owner, step, senders)
        data_copy(target, owner).start()
        meta_copy(target, owner).start()
        return carry

    lax.fori_loop(1, senders, start_all, 0)
    loads[0].wait()
    for target in others:
        weight_copy(target, mine).start()
    own_w = pltpu.make_async_copy(
        w_mat.at[:, pl.ds(pl.multiple_of(mine * part, part), part)], w_cols.at[mine], local_sem.at[0]
    )
    own_w.start()
    own_meta = pltpu.make_async_copy(
        meta.at[rows_of(owner, 8), :], slots_in.at[rows_of(owner, 8), :], local_sem.at[1]
    )
    own_meta.start()

    def project(parts, source):
        values = jnp.concatenate(parts, axis=1).astype(jnp.float32)
        centred = values - jnp.sum(values, axis=-1, keepdims=True) * (1.0 / width)
        spread_of = jnp.sum(centred * centred, axis=-1, keepdims=True) * (1.0 / width)
        normed = (centred * lax.rsqrt(spread_of + EPSILON)).astype(jnp.bfloat16)
        here = pl.ds(source * block_tiles, block_tiles)
        for weight, result in ((q_mat, q_out), (k_mat, k_out), (v_mat, v_out)):
            product = jnp.dot(normed, weight[...], preferred_element_type=jnp.float32)
            result[here] = product.astype(jnp.bfloat16).reshape(block_tiles, tile, part)

    def spread(source):
        share(mine, source, across, far_send, far_recv).start()
        share(mine, source, sibling, sib_send, sib_recv).start()

    def relay(source):
        share(across, source, across, far_send, far_recv).wait_recv()
        share(across, source, sibling, fwd_send, fwd_recv).start()

    other = lax.rem(sibling + splits // 2, splits)

    def source_at(step):
        return paired(owner, step, senders)

    def compute(source):
        share(sibling, source, sibling, sib_send, sib_recv).wait_recv()
        share(other, source, sibling, fwd_send, fwd_recv).wait_recv()
        here = rows_of(source, block)
        project([gathered[p, here, :] for p in range(splits)], source)
        own_out[pl.ds(source * block_tiles, block_tiles)] = gathered[mine, here, :].reshape(
            block_tiles, tile, part
        )

    for load in loads[1:]:
        load.wait()
    project([kept[...]], owner)
    own_out[pl.ds(owner * block_tiles, block_tiles)] = outgoing[rows_of(owner, block), :].reshape(
        block_tiles, tile, part
    )

    def arrive(step, carry):
        source = source_at(step)
        data_copy(owner, source).wait_recv()
        spread(source)

        @pl.when(step >= 2)
        def _():
            relay(source_at(step - 1))

        @pl.when(step >= 3)
        def _():
            compute(source_at(step - 2))

        return carry

    lax.fori_loop(1, senders, arrive, 0)
    relay(source_at(senders - 1))

    def compute_rest(step, carry):
        compute(source_at(step))
        return carry

    lax.fori_loop(max(1, senders - 2), senders, compute_rest, 0)
    own_w.wait()
    own_meta.wait()
    for target in others:
        weight_copy(mine, target).wait_recv()
        weight_copy(target, mine).wait_send()

    def finish(step, carry):
        source = source_at(step)
        share(mine, source, across, far_send, far_recv).wait_send()
        share(mine, source, sibling, sib_send, sib_recv).wait_send()
        share(across, source, sibling, fwd_send, fwd_recv).wait_send()
        return carry

    lax.fori_loop(1, senders, finish, 0)

    def finish_peers(step, carry):
        source = source_at(step)
        target = source
        meta_copy(owner, source).wait_recv()
        meta_copy(target, owner).wait_send()
        data_copy(target, owner).wait_send()
        return carry

    lax.fori_loop(1, senders, finish_peers, 0)
    slots = rows // tile
    rank = lax.broadcasted_iota(jnp.int32, (128, slots), 0)
    target_slot = lax.broadcasted_iota(jnp.int32, (128, slots), 1)

    def locate(source, total):
        line = slots_in[rows_of(source, 8), :].astype(jnp.float32)[0:1, :]
        placed = jnp.broadcast_to(line, (128, 128)).T[:, 0:1].astype(jnp.int32)
        found = (placed == target_slot) & (rank < block_tiles)
        position = jnp.where(found, rank + source * block_tiles, 0)
        return total + jnp.sum(position, axis=0, keepdims=True)

    arrived[...] = lax.fori_loop(0, senders, locate, jnp.zeros((1, slots), jnp.int32))


def exchange(outgoing, meta, kept, w_query, w_key, w_value, w_out, senders, splits, tile):
    rows, part = outgoing.shape
    kind = outgoing.dtype
    dma = pltpu.SemaphoreType.DMA
    tiles = jax.ShapeDtypeStruct((rows // tile, tile, part), kind)
    return pl.pallas_call(
        functools.partial(exchange_kernel, senders, splits, tile),
        out_shape=[
            tiles,
            tiles,
            tiles,
            tiles,
            jax.ShapeDtypeStruct((1, rows // tile), meta.dtype),
            jax.ShapeDtypeStruct((splits, part, part), kind),
        ],
        in_specs=[VMEM] * 3 + [pl.BlockSpec(memory_space=pl.ANY)] * 4,
        out_specs=[VMEM] * 6,
        scratch_shapes=[
            pltpu.VMEM((splits, rows, part), kind),
            pltpu.VMEM(meta.shape, meta.dtype),
            pltpu.VMEM(w_query.shape, kind),
            pltpu.VMEM(w_key.shape, kind),
            pltpu.VMEM(w_value.shape, kind),
            pltpu.VMEM(w_out.shape, kind),
            dma((4,)),
            dma((splits,)),
            dma((splits,)),
        ]
        + [dma((senders,))] * 10
        + [dma((2,))],
        compiler_params=pltpu.CompilerParams(
            collective_id=0, has_side_effects=True, vmem_limit_bytes=LIMIT
        ),
        name="exchange",
    )(outgoing, meta, kept, w_query, w_key, w_value, w_out)


def attend_kernel(
    senders, splits, arrived, q_in, k_in, v_in, own_in, w_cols, image, out, pooled_out,
    q_ref, k_ref, v_ref, own, segments, att, tile_sums, message, inbox,
    sib_send, sib_recv, far_send, far_recv, fwd_send, fwd_recv, sum_send, sum_recv,
):
    owner = lax.axis_index("dp")
    mine, sibling, across = partners(splits)
    other = lax.rem(sibling + splits // 2, splits)
    rows, part = k_ref.shape
    slots, tile, _ = k_in.shape
    q_rows = Q_TILES * tile
    window = q_rows + 2 * MAX_TILES * tile
    chunk = q_rows
    chunks = rows // chunk
    pairs = part // 128
    others = [lax.rem(mine + step, splits) for step in range(1, splits)]
    greet(senders, others)

    def share(group, index, peer, send_sem, recv_sem):
        view = att.at[group, rows_of(index, chunk), :]
        return pltpu.make_async_remote_copy(
            src_ref=view,
            dst_ref=view,
            send_sem=send_sem.at[index],
            recv_sem=recv_sem.at[index],
            device_id={"mp": peer},
        )

    def spread(index):
        share(mine, index, across, far_send, far_recv).start()
        share(mine, index, sibling, sib_send, sib_recv).start()

    def relay(index):
        share(across, index, across, far_send, far_recv).wait_recv()
        share(across, index, sibling, fwd_send, fwd_recv).start()

    low = lax.broadcasted_iota(jnp.int32, (q_rows, 128), 1) < HEAD_DIM

    zero = jnp.zeros((tile, 128), jnp.bfloat16)
    low_tile = lax.broadcasted_iota(jnp.int32, (tile, 128), 1) < HEAD_DIM

    def permute(block, carry):
        for t in range(Q_TILES):
            place = arrived[0, block * Q_TILES + t]
            here = rows_of(block * Q_TILES + t, tile)
            query = q_in[place]
            value = v_in[place]
            k_ref[here, :] = k_in[place]
            own[here, :] = own_in[place]
            for p in range(pairs):
                pair = query[:, p * 128 : (p + 1) * 128]
                base = block * 2 * Q_TILES + t
                q_ref[p, rows_of(base, tile), :] = jnp.where(low_tile, pair, zero)
                q_ref[p, rows_of(base + Q_TILES, tile), :] = jnp.where(low_tile, zero, pair)
                v_ref[here, p * 256 : p * 256 + 128] = value[:, p * 128 : (p + 1) * 128]
                v_ref[here, p * 256 + 128 : (p + 1) * 256] = jnp.ones((tile, 128), jnp.bfloat16)
        return carry

    lax.fori_loop(0, slots // Q_TILES, permute, 0)
    spans = lax.broadcasted_iota(jnp.int32, (slots, rows), 1) // tile
    expand = (spans == lax.broadcasted_iota(jnp.int32, (slots, rows), 0)).astype(jnp.bfloat16)
    numbers = jnp.broadcast_to(image[...].astype(jnp.float32), (8, slots)).astype(jnp.bfloat16)
    segments[...] = jnp.dot(numbers, expand, preferred_element_type=jnp.float32)

    def attend(block):
        start = jnp.clip(block * q_rows - MAX_TILES * tile, 0, rows - window)
        across_rows = segments[0:1, rows_of(block, q_rows)]
        of_query = jnp.broadcast_to(across_rows, (q_rows, q_rows)).T[:, 0:1]
        of_key = segments[0:1, pl.ds(pl.multiple_of(start, q_rows), window)]
        bias = jnp.where(of_query == of_key, 0.0, -1e30)
        keys = pl.ds(pl.multiple_of(start, q_rows), window)
        for p in range(pairs):
            queries = q_ref[p, rows_of(block, 2 * q_rows), :]
            key_rows = k_ref[keys, p * 128 : (p + 1) * 128]
            values = v_ref[keys, p * 256 : (p + 1) * 256]
            scores = lax.dot_general(
                queries, key_rows, (((1,), (1,)), ((), ())), preferred_element_type=jnp.float32
            )
            halves = []
            for half in range(2):
                masked = scores[half * q_rows : (half + 1) * q_rows, :] * HEAD_DIM**-0.5 + bias
                peak = jnp.max(masked, axis=-1, keepdims=True)
                raised = jnp.exp(masked - peak).astype(jnp.bfloat16)
                mixed = jnp.dot(raised, values, preferred_element_type=jnp.float32)
                halves.append(mixed[:, :128] / mixed[:, 128:])
            att[mine, rows_of(block, q_rows), p * 128 : (p + 1) * 128] = jnp.where(
                low, halves[0], halves[1]
            ).astype(jnp.bfloat16)

    live = jnp.sum((image[...] >= 0).astype(jnp.int32), axis=1, keepdims=True) * tile
    relay_lag = min(6, chunks)
    output_lag = min(8, chunks)

    def output(index):
        share(sibling, index, sibling, sib_send, sib_recv).wait_recv()
        share(other, index, sibling, fwd_send, fwd_recv).wait_recv()
        here = rows_of(index, chunk)
        total = jnp.zeros((chunk, part), jnp.float32)
        for group in range(splits):
            term = jnp.dot(att[group, here, :], w_cols[group], preferred_element_type=jnp.float32)
            total = total + term.astype(jnp.bfloat16).astype(jnp.float32)
        row = lax.broadcasted_iota(jnp.int32, (chunk, 1), 0) + index * chunk
        result = jnp.where(row < live, own[here, :].astype(jnp.float32) + total, 0.0)
        out[here, :] = result.astype(jnp.bfloat16)
        tile_sums[rows_of(index, chunk // tile), :] = jnp.sum(
            result.reshape(chunk // tile, tile, part), axis=1
        )

    def attention_step(index, carry):
        attend(index)

        @pl.when(index >= 1)
        def _():
            spread(index - 1)

        @pl.when(index >= relay_lag)
        def _():
            relay(index - relay_lag)

        @pl.when(index >= output_lag)
        def _():
            output(index - output_lag)

        return carry

    lax.fori_loop(0, chunks, attention_step, 0)
    spread(chunks - 1)

    def output_step(index, carry):
        @pl.when(index < chunks - output_lag + relay_lag)
        def _():
            relay(index + output_lag - relay_lag)

        output(index)
        return carry

    lax.fori_loop(chunks - output_lag, chunks - output_lag + relay_lag, output_step, 0)

    def rest(index, carry):
        output(index)
        return carry

    lax.fori_loop(chunks - output_lag + relay_lag, chunks, rest, 0)
    labels = lax.broadcasted_iota(jnp.int32, (IMG_OWN, slots), 0)
    member = (image[...] == labels).astype(jnp.float32)
    sums = jnp.dot(
        member, tile_sums[...], precision=lax.Precision.HIGHEST, preferred_element_type=jnp.float32
    )
    image_rows = jnp.sum(member, axis=1, keepdims=True) * float(tile)
    filled = image_rows > 0
    pooled = sums / jnp.maximum(image_rows, 1.0)
    local_sum = jnp.sum(jnp.where(filled, pooled, 0.0), axis=0, keepdims=True)
    local_count = jnp.sum(filled.astype(jnp.float32), axis=0, keepdims=True)
    message[:, :part] = jnp.broadcast_to(local_sum, (8, part))
    message[:, part:] = jnp.broadcast_to(local_count, (8, 128))

    def drain(index, carry):
        share(mine, index, across, far_send, far_recv).wait_send()
        share(mine, index, sibling, sib_send, sib_recv).wait_send()
        share(across, index, sibling, fwd_send, fwd_recv).wait_send()
        return carry

    lax.fori_loop(0, chunks, drain, 0)
    def sum_copy(target, source):
        return pltpu.make_async_remote_copy(
            src_ref=message,
            dst_ref=inbox.at[source],
            send_sem=sum_send.at[target],
            recv_sem=sum_recv.at[source],
            device_id={"dp": target},
        )

    def send_sum(step, carry):
        sum_copy(lax.rem(owner + step, senders), owner).start()
        return carry

    lax.fori_loop(1, senders, send_sum, 0)
    inbox[owner] = message[...]

    def wait_sum(step, carry):
        sum_copy(owner, lax.rem(owner + senders - step, senders)).wait_recv()
        sum_copy(lax.rem(owner + step, senders), owner).wait_send()
        return carry

    lax.fori_loop(1, senders, wait_sum, 0)
    grand = lax.fori_loop(
        0, senders, lambda i, acc: acc + inbox[i], jnp.zeros(message.shape, jnp.float32)
    )
    centre = grand[0:1, :part] / grand[0:1, part : part + 1]
    pooled_out[...] = jnp.where(filled, pooled - centre, 0.0).astype(jnp.bfloat16)


def finish_block(arrived, queries, keys, values, own, w_cols, image, senders, splits):
    slots, tile, part = keys.shape
    rows = slots * tile
    chunks = slots // Q_TILES
    kind = keys.dtype
    dma = pltpu.SemaphoreType.DMA
    return pl.pallas_call(
        functools.partial(attend_kernel, senders, splits),
        out_shape=[
            jax.ShapeDtypeStruct((rows, part), kind),
            jax.ShapeDtypeStruct((IMG_OWN, part), kind),
        ],
        in_specs=[SMEM] + [VMEM] * 6,
        out_specs=[VMEM, VMEM],
        scratch_shapes=[
            pltpu.VMEM((part // 128, 2 * rows, 128), kind),
            pltpu.VMEM((rows, part), kind),
            pltpu.VMEM((rows, 2 * part), kind),
            pltpu.VMEM((rows, part), kind),
            pltpu.VMEM((8, rows), jnp.float32),
            pltpu.VMEM((splits, rows, part), kind),
            pltpu.VMEM((slots, part), jnp.float32),
            pltpu.VMEM((8, part + 128), jnp.float32),
            pltpu.VMEM((senders, 8, part + 128), jnp.float32),
        ]
        + [dma((chunks,))] * 6
        + [dma((senders,))] * 2,
        compiler_params=pltpu.CompilerParams(
            collective_id=1, has_side_effects=True, vmem_limit_bytes=LIMIT
        ),
        name="attend",
    )(arrived, queries, keys, values, own, w_cols, image)


def hand_kernel(rows, pooled, rows_out, pooled_out):
    rows_out[...] = rows[...]
    pooled_out[...] = pooled[...]


def hand_over(rows, pooled):
    steps = 2
    big = pl.BlockSpec((rows.shape[0] // steps, rows.shape[1]), lambda i: (i, 0))
    small = pl.BlockSpec(pooled.shape, lambda i: (0, 0))
    return pl.pallas_call(
        hand_kernel,
        grid=(steps,),
        out_shape=[
            jax.ShapeDtypeStruct(rows.shape, rows.dtype),
            jax.ShapeDtypeStruct(pooled.shape, pooled.dtype),
        ],
        in_specs=[big, small],
        out_specs=[big, small],
        name="hand_over",
    )(rows, pooled)


def on_device(patches, dest_owner, dest_slot, packed_image, w_query, w_key, w_value, w_out):
    senders = lax.axis_size("dp")
    splits = lax.axis_size("mp")
    slots = dest_owner.shape[0]
    tile = patches.shape[0] // slots
    outgoing, meta, kept = pack(dest_owner, dest_slot, patches, senders, splits)
    queries, keys, values, own, arrived, w_cols = exchange(
        outgoing, meta, kept, w_query, w_key, w_value, w_out, senders, splits, tile
    )
    packed_out, pooled_out = finish_block(
        arrived, queries, keys, values, own, w_cols, packed_image[None, :], senders, splits
    )
    return hand_over(packed_out, pooled_out)


def solution(mesh):
    in_specs = (
        P("dp", None),
        P("dp"),
        P("dp"),
        P("dp"),
        P(None, "mp"),
        P(None, "mp"),
        P(None, "mp"),
        P("mp", None),
    )
    out_specs = (P("dp", "mp"), P("dp", "mp"))
    return jax.shard_map(
        on_device, mesh=mesh, in_specs=in_specs, out_specs=out_specs, check_vma=False
    )
```
